512 devices in a mesh: seq: 128 (over x, y, z_lo, core), head: 4 (over z_hi).
Axes of the slice: x: 4, y: 8, z: 8 (z_hi: 4, z_lo: 2; z = z_hi * 2 + z_lo), core: 2. Of those that a mesh axis runs over, the one named last changes fastest.
Arguments:
- queries: bfloat16 [128, 8192], P('seq', 'head'), may hold values from -130 to 130
- grad_output: bfloat16 [128, 8192], P('seq', 'head'), may hold values from -384 to 384
- key_cache: bfloat16 [49152, 512], P('seq', 'head'), may hold values from -6 to 6
- saved_value_rows: bfloat16 [49152, 512], P('seq', 'head'), may hold values from -6 to 6
- lengths: int32 [128], P('seq'), may hold values from 1 to 384, 36864 in all
- span_index: int32 [1], replicated, may hold values from 72 to 287
- w_query: bfloat16 [4096, 8192], P('seq', 'head'), may hold values from -0.09375 to 0.09375
- key_projection_weight: bfloat16 [4096, 512], P(None, 'head'), may hold values from -0.09375 to 0.09375
- value_projection_weight: bfloat16 [4096, 512], P(None, 'head'), may hold values from -0.09375 to 0.09375
Outputs:
- saved_key_gradient: bfloat16 [49152, 512], P('seq', 'head')
- saved_value_gradient: bfloat16 [49152, 512], P('seq', 'head')
- cached_input_gradient: bfloat16 [49152, 4096], P('seq', 'head')
- grad_span_input: bfloat16 [128, 4096], P('head', 'seq')
The draws below stay inside these ranges and needn't reach their ends.
All inputs are finite; a program needn't handle non-finite values. No bound on the sum of `lengths` on one device may be relied on, other than what follows from the above.
Results may differ from the reference program's by a relative error of at most 0.02.
Values may be sent and summed in bfloat16 or wider, within the bound.
No kernel may reach another device: no remote copies, remote signals or barrier semaphores. Data moves between devices by JAX's collectives and lax.ppermute only.
A program may use at most 64 MiB of HBM per device.

```python
import math
import jax
import jax.numpy as jnp
import numpy as np
from jax import lax

MODEL_WIDTH = 4096
QUERY_HEADS = 64
KEY_VALUE_HEADS = 4
HEAD_WIDTH = 128
QC = 128
OWNER_SLOTS = 384
TOTAL_SLOTS = 49152
LIVE = 36864
N_SEQ = 128


def cache_row_list(key):
    sampled_values = jnp.clip(jax.random.normal(jax.random.fold_in(key, 11), (TOTAL_SLOTS, KEY_VALUE_HEADS * HEAD_WIDTH), jnp.float32), -5.0, 5.0)
    return sampled_values


def draw_key_cache(key, part):
    return cache_row_list(key).astype(jnp.bfloat16)


def draw_queries(key, part):
    sampled_values = jnp.clip(jax.random.normal(jax.random.fold_in(key, 23), (QC, QUERY_HEADS * HEAD_WIDTH), jnp.float32), -5.0, 5.0)
    return sampled_values.astype(jnp.bfloat16)


def shard_levels(own_key, extent, pieces, smallest, top_value):
    def one(dim, parts):
        steps = jax.random.uniform(jax.random.fold_in(jax.random.fold_in(own_key, 6), dim), (parts,), jnp.float32, smallest / len(pieces), top_value / len(pieces))
        return jnp.repeat(jnp.exp(steps), extent[dim] // parts).reshape((-1,) + (1,) * (len(extent) - dim - 1))

    factor_of = one(*pieces[0])
    for cut in pieces[1:]:
        factor_of = factor_of * one(*cut)
    return factor_of


def profile(count, total, bound, skew):
    portions = [(1 << 20) // math.isqrt(rank ** skew) + 1 for rank in range(2, count + 1)]
    surplus, counts = total - bound - (count - 1), [1] * (count - 1)
    while surplus > 0:
        movable = [i for i in range(count - 1) if counts[i] < bound]
        pool, remaining = sum([portions[i] for i in movable]), surplus
        for i in movable:
            addition = min(bound - counts[i], max(1, remaining * portions[i] // pool), surplus)
            counts[i] = counts[i] + addition
            surplus = surplus - addition
    return np.array([bound] + counts)


def uneven(key, amount, total, reach, slope):
    if amount == 2:
        one = jax.random.randint(key, (), max(1, total - reach), min(reach, total - 1) + 1)
        return jnp.stack([one, total - one])
    tallies = jnp.asarray(profile(amount, total, reach, slope), jnp.int32)
    pairs = (amount - 1) // 2
    donor, sink = tallies[1:1 + 2 * pairs:2], tallies[2:2 + 2 * pairs:2]
    room = jnp.minimum(donor - 1, reach - sink)
    moved = jax.random.randint(jax.random.fold_in(key, 1), (pairs,), 0, 1 << 20) % (room + 1)
    tallies = tallies.at[1:1 + 2 * pairs:2].set(donor - moved).at[2:2 + 2 * pairs:2].set(sink + moved)
    return tallies[jax.random.permutation(jax.random.fold_in(key, 2), amount)]


def gaussian(stream_key, extent, scale, most, shards=(), kind=jnp.bfloat16):
    entries = scale * jax.random.normal(stream_key, extent, jnp.float32)
    if shards:
        entries = entries * shard_levels(stream_key, extent, shards, -0.22, 0.18)
    return jnp.clip(entries, -most, most).astype(kind)


def setup_inputs(seed: int = 0) -> dict:
    streams_of = jax.random.split(jax.random.key(seed), 10)
    queries = draw_queries(jax.random.fold_in(streams_of[9], 71), 0)
    grad_output = gaussian(streams_of[1], (QC, QUERY_HEADS * HEAD_WIDTH), 64.0, 384.0, ((0, 128), (1, 4)))
    key_cache = draw_key_cache(jax.random.fold_in(streams_of[9], 71), 0)
    saved_value_rows = gaussian(streams_of[3], (TOTAL_SLOTS, KEY_VALUE_HEADS * HEAD_WIDTH), 1.0, 6.0, ((0, 128), (1, 4)))
    lengths = uneven(streams_of[4], N_SEQ, LIVE, OWNER_SLOTS, 2).astype(jnp.int32)
    span_index = jax.random.randint(streams_of[5], (1,), LIVE // (4 * QC), LIVE // QC).astype(jnp.int32)
    w_query = gaussian(streams_of[6], (MODEL_WIDTH, QUERY_HEADS * HEAD_WIDTH), MODEL_WIDTH ** -0.5, 0.09375, ((0, 128), (1, 4)))
    key_projection_weight = gaussian(streams_of[7], (MODEL_WIDTH, KEY_VALUE_HEADS * HEAD_WIDTH), MODEL_WIDTH ** -0.5, 0.09375, ((1, 4),))
    value_projection_weight = gaussian(streams_of[8], (MODEL_WIDTH, KEY_VALUE_HEADS * HEAD_WIDTH), MODEL_WIDTH ** -0.5, 0.09375, ((1, 4),))
    return dict(queries=queries, grad_output=grad_output, key_cache=key_cache, saved_value_rows=saved_value_rows, lengths=lengths, span_index=span_index, w_query=w_query, key_projection_weight=key_projection_weight, value_projection_weight=value_projection_weight)


LOWEST_SCORE = -1.0e30


def head_backward(query_rows, output_grads, key_block, value_block, visible):
    score_scale = HEAD_WIDTH ** -0.5
    scores = jnp.dot(query_rows, key_block.T, preferred_element_type=jnp.float32) * score_scale
    row_peak = jnp.max(jnp.where(visible, scores, LOWEST_SCORE), axis=1, keepdims=True)
    exponentials = jnp.exp(jnp.where(visible, scores - row_peak, LOWEST_SCORE))
    weights = exponentials / jnp.sum(exponentials, axis=1, keepdims=True)
    weight_grads = jnp.dot(output_grads, value_block.T, preferred_element_type=jnp.float32)
    row_terms = jnp.sum(weights * weight_grads, axis=1, keepdims=True)
    score_grads = weights * (weight_grads - row_terms)
    weights_low = weights.astype(jnp.bfloat16)
    score_low = score_grads.astype(jnp.bfloat16)
    value_grads = jnp.dot(weights_low.T, output_grads, preferred_element_type=jnp.float32)
    key_grads = jnp.dot(score_low.T, query_rows, preferred_element_type=jnp.float32)
    query_grads = jnp.dot(score_low, key_block, preferred_element_type=jnp.float32) * score_scale
    return query_grads, key_grads, value_grads


def reference(queries, grad_output, key_cache, saved_value_rows, lengths, span_index, w_query, key_projection_weight, value_projection_weight):
    heads_per_group = QUERY_HEADS // KEY_VALUE_HEADS
    slot_count = key_cache.shape[0]
    offsets = (jnp.cumsum(lengths) - lengths).astype(jnp.int32)
    slot_ids = jnp.arange(slot_count, dtype=jnp.int32)
    owners = slot_ids // OWNER_SLOTS
    within = slot_ids - owners * OWNER_SLOTS
    positions = offsets[owners] + within
    query_positions = span_index[0] * QC + jnp.arange(QC, dtype=jnp.int32)
    visible = (within < lengths[owners])[None, :] & (positions[None, :] <= query_positions[:, None])
    query_parts = []
    key_parts = []
    value_parts = []
    for shared_key_head in range(KEY_VALUE_HEADS):
        first = shared_key_head * HEAD_WIDTH
        key_block = key_cache[:, first:first + HEAD_WIDTH]
        value_block = saved_value_rows[:, first:first + HEAD_WIDTH]
        start = shared_key_head * heads_per_group * HEAD_WIDTH
        query_heads = queries[:, start:start + heads_per_group * HEAD_WIDTH].reshape(QC, heads_per_group, HEAD_WIDTH).transpose(1, 0, 2)
        grad_heads = grad_output[:, start:start + heads_per_group * HEAD_WIDTH].reshape(QC, heads_per_group, HEAD_WIDTH).transpose(1, 0, 2)

        def one_head(carry, pair, key_block=key_block, value_block=value_block):
            query_grads, key_grads, value_grads = head_backward(pair[0], pair[1], key_block, value_block, visible)
            return (carry[0] + key_grads, carry[1] + value_grads), query_grads

        zero_sums = jnp.zeros((slot_count, HEAD_WIDTH), jnp.float32)
        (key_sum, value_sum), query_grads = lax.scan(one_head, (zero_sums, zero_sums), (query_heads, grad_heads))
        query_parts.append(query_grads.transpose(1, 0, 2).reshape(QC, heads_per_group * HEAD_WIDTH))
        key_parts.append(key_sum * (HEAD_WIDTH ** -0.5))
        value_parts.append(value_sum)
    saved_key_gradient = jnp.concatenate(key_parts, axis=1).astype(jnp.bfloat16)
    saved_value_gradient = jnp.concatenate(value_parts, axis=1).astype(jnp.bfloat16)
    query_low = jnp.concatenate(query_parts, axis=1).astype(jnp.bfloat16)
    grad_span_input = jnp.dot(query_low, w_query.T, preferred_element_type=jnp.float32).astype(jnp.bfloat16)
    joined_weights = []
    for shared_key_head in range(KEY_VALUE_HEADS):
        first = shared_key_head * HEAD_WIDTH
        joined_weights.append(jnp.concatenate([key_projection_weight[:, first:first + HEAD_WIDTH], value_projection_weight[:, first:first + HEAD_WIDTH]], axis=1))

    def owner_slot_block(pair):
        key_rows, value_rows = pair
        total = jnp.zeros((OWNER_SLOTS, MODEL_WIDTH), jnp.float32)
        for shared_key_head in range(KEY_VALUE_HEADS):
            first = shared_key_head * HEAD_WIDTH
            both = jnp.concatenate([key_rows[:, first:first + HEAD_WIDTH], value_rows[:, first:first + HEAD_WIDTH]], axis=1)
            partial_term = jnp.dot(both, joined_weights[shared_key_head].T, preferred_element_type=jnp.float32)
            rounded = lax.optimization_barrier(partial_term.astype(jnp.bfloat16))
            total = total + rounded.astype(jnp.float32)
        return total.astype(jnp.bfloat16)

    cached_input_gradient = lax.map(owner_slot_block, (saved_key_gradient.reshape(N_SEQ, OWNER_SLOTS, KEY_VALUE_HEADS * HEAD_WIDTH), saved_value_gradient.reshape(N_SEQ, OWNER_SLOTS, KEY_VALUE_HEADS * HEAD_WIDTH)))
    cached_input_gradient = cached_input_gradient.reshape(slot_count, MODEL_WIDTH)
    return (saved_key_gradient, saved_value_gradient, cached_input_gradient, grad_span_input)
```

```python
import functools

import jax
import jax.numpy as jnp
from jax import lax
from jax.experimental import pallas as pl
from jax.experimental.pallas import tpu as pltpu
from jax.sharding import Mesh
from jax.sharding import PartitionSpec as P

HEAD_WIDTH = 128
SEQ = ("seq_0", "seq_1", "seq_2", "seq_3")
FAR = ("seq_0", "seq_1", "seq_2")
CORE = "seq_3"
LOWEST_SCORE = -1e30
LOWEST_PEAK = -1e29
DEAD = 1e9
SCALE = HEAD_WIDTH ** (-0.5)
F32 = jnp.float32
BF16 = jnp.bfloat16
VMEM = pl.BlockSpec(memory_space=pltpu.VMEM)
SMEM = pl.BlockSpec(memory_space=pltpu.SMEM)


def rows_dot(a, b):
    return lax.dot_general(a, b, (((1,), (1,)), ((), ())), preferred_element_type=F32)


def plain_dot(a, b):
    return lax.dot_general(a, b, (((1,), (0,)), ((), ())), preferred_element_type=F32)


def three_parts(value):
    high = value.astype(BF16)
    rest = value - high.astype(F32)
    middle = rest.astype(BF16)
    low = (rest - middle.astype(F32)).astype(BF16)
    return high, middle, low


def packed_stats(columns, lanes):
    count = len(columns)
    rows = columns[0].shape[0]
    lane = lax.broadcasted_iota(jnp.int32, (rows, 128), 1)
    held = jnp.zeros((rows, 128), F32)
    for k, column in enumerate(columns):
        held = jnp.where(lane == k, column, held)
    return parts_side_by_side(held, count, lanes)


def parts_side_by_side(held, count, lanes):
    parts = [part[:, :count].astype(F32) for part in three_parts(held)]
    joined = jnp.concatenate(parts, axis=1)
    spare = jnp.zeros((held.shape[0], lanes - joined.shape[1]), F32)
    return jnp.concatenate([joined, spare], axis=1).astype(BF16)


def unpacked_stats(block, count):
    wide = block.astype(F32)
    return wide[:, :count] + wide[:, count : 2 * count] + wide[:, 2 * count : 3 * count]


def first_kernel(heads, group, where_ref, x_ref, k_ref, v_ref, y_ref, place_ref):
    rows = x_ref.shape[0]
    slots = k_ref.shape[0]
    half = slots // 2
    width = heads * HEAD_WIDTH
    far, core, span, row_total = (where_ref[0], where_ref[1], where_ref[2], where_ref[3])
    lens = x_ref[:, 2 * width : 2 * width + 128].astype(F32)
    lane = lax.broadcasted_iota(jnp.int32, (rows, 128), 1)
    row = lax.broadcasted_iota(jnp.int32, (rows, 128), 0)
    weight = jnp.where((lane == 0) | (lane == 2), 16.0, jnp.where((lane == 1) | (lane == 3), 1.0, 0.0))
    lens = lens * weight
    base = jnp.sum(jnp.where(row < far, lens, 0.0))
    here = jnp.where(row == far, lens, 0.0)
    own = jnp.sum(jnp.where(lane < 2, here, 0.0))
    other = jnp.sum(jnp.where(lane >= 2, here, 0.0))
    is_second = core.astype(F32)
    own_offset = base + is_second * other
    other_offset = base + (1.0 - is_second) * own
    place_ref[0] = own_offset
    place_ref[1] = other_offset
    place_ref[2] = own
    place_ref[3] = other
    within = lax.broadcasted_iota(jnp.int32, (1, half), 1).astype(F32)
    position = jnp.concatenate(
        [
            jnp.where(within < own, own_offset + within, DEAD),
            jnp.where(within < other, other_offset + within, DEAD),
        ],
        axis=1,
    )
    tall = group * rows
    index = lax.broadcasted_iota(jnp.int32, (tall, 1), 0) % rows
    asked = (span * row_total + 2 * index + core).astype(F32)
    visible = position <= asked
    keys = k_ref[...]
    values = v_ref[...]
    peaks, totals, means = [], [], []
    for first in range(0, heads, group):
        at = [(first + k) * HEAD_WIDTH for k in range(group)]
        q = jnp.concatenate([x_ref[:, a : a + HEAD_WIDTH] for a in at], axis=0)
        g = jnp.concatenate([x_ref[:, width + a : width + a + HEAD_WIDTH] for a in at], axis=0)
        scores = jnp.where(visible, rows_dot(q, keys) * SCALE, LOWEST_SCORE)
        peak = jnp.maximum(jnp.max(scores, axis=1, keepdims=True), LOWEST_PEAK)
        raised = jnp.exp(scores - peak)
        grads = rows_dot(g, values)
        total = jnp.sum(raised, axis=1, keepdims=True)
        mean = jnp.sum(raised * grads, axis=1, keepdims=True) / jnp.maximum(total, 0.5)
        moved = (raised * (grads - mean)).astype(BF16)
        both = plain_dot(jnp.concatenate([moved, raised.astype(BF16)], axis=0), keys)
        for k, a in enumerate(at):
            y_ref[:, a : a + HEAD_WIDTH] = both[k * rows : (k + 1) * rows].astype(BF16)
            y_ref[:, width + a : width + a + HEAD_WIDTH] = both[
                tall + k * rows : tall + (k + 1) * rows
            ].astype(BF16)
            peaks.append(peak[k * rows : (k + 1) * rows])
            totals.append(total[k * rows : (k + 1) * rows])
            means.append(mean[k * rows : (k + 1) * rows])
    y_ref[:, 2 * width :] = packed_stats(peaks + totals + means, 256)


def merge_kernel(heads, z_ref, u_ref):
    width = heads * HEAD_WIDTH
    count = u_ref.shape[0]
    stats = unpacked_stats(z_ref[:, 2 * width :], 3 * heads)
    peak, total, mean = (
        stats[:, :heads],
        stats[:, heads : 2 * heads],
        stats[:, 2 * heads : 3 * heads],
    )
    row_peak = jnp.max(peak, axis=0, keepdims=True)
    share = jnp.exp(peak - row_peak)
    part = share * total
    row_total = jnp.sum(part, axis=0, keepdims=True)
    row_mean = jnp.sum(part * mean, axis=0, keepdims=True) / row_total
    moved_factor = share * (SCALE / row_total)
    plain_factor = moved_factor * (mean - row_mean)
    for h in range(heads):
        a = h * HEAD_WIDTH
        term = z_ref[:, a : a + HEAD_WIDTH].astype(F32) * moved_factor[:, h : h + 1]
        term += z_ref[:, width + a : width + a + HEAD_WIDTH].astype(F32) * plain_factor[:, h : h + 1]
        line = jnp.sum(term, axis=0, keepdims=True)
        u_ref[:, a : a + HEAD_WIDTH] = jnp.broadcast_to(line, (count, HEAD_WIDTH)).astype(BF16)
    found = jnp.concatenate(
        [row_peak, row_total, row_mean, jnp.zeros((1, 128 - 3 * heads), F32)], axis=1
    )
    packed = parts_side_by_side(jnp.broadcast_to(found, (count, 128)), 3 * heads, 256)
    u_ref[:, width:] = packed


def second_kernel(heads, where_ref, place_ref, x_ref, u_ref, k_ref, v_ref, own_ref, other_ref):
    rows = x_ref.shape[0]
    slots = k_ref.shape[0]
    half = slots // 2
    width = heads * HEAD_WIDTH
    core, span, row_total = (where_ref[1], where_ref[2], where_ref[3])
    within = lax.broadcasted_iota(jnp.int32, (half, 1), 0).astype(F32)
    position = jnp.concatenate(
        [
            jnp.where(within < place_ref[2], place_ref[0] + within, DEAD),
            jnp.where(within < place_ref[3], place_ref[1] + within, DEAD),
        ],
        axis=0,
    )
    index = lax.broadcasted_iota(jnp.int32, (1, 2 * rows), 1) % rows
    asked = (span * row_total + 2 * index + core).astype(F32)
    visible = position <= asked
    stats = unpacked_stats(u_ref[:, width:], 3 * heads)
    stats = jnp.concatenate([stats, jnp.zeros((rows, 128 - 3 * heads), F32)], axis=1)
    turned = jnp.transpose(stats)
    keys = k_ref[...]
    values = v_ref[...]
    value_grads = jnp.zeros((slots, HEAD_WIDTH), F32)
    key_grads = jnp.zeros((slots, HEAD_WIDTH), F32)

    def of_pair(kind, h):
        line = kind * heads + h
        return jnp.concatenate([turned[line : line + 1], turned[line + 1 : line + 2]], axis=1)

    for h in range(0, heads, 2):
        a = h * HEAD_WIDTH
        q = jnp.concatenate(
            [x_ref[:, a : a + HEAD_WIDTH], x_ref[:, a + HEAD_WIDTH : a + 2 * HEAD_WIDTH]], axis=0
        )
        a += width
        g = jnp.concatenate(
            [x_ref[:, a : a + HEAD_WIDTH], x_ref[:, a + HEAD_WIDTH : a + 2 * HEAD_WIDTH]], axis=0
        )
        scores = rows_dot(keys, q) * SCALE
        raised = jnp.exp(jnp.where(visible, scores - of_pair(0, h), LOWEST_SCORE))
        weights = raised * (1.0 / of_pair(1, h))
        score_grads = weights * (rows_dot(values, g) - of_pair(2, h))
        value_grads += plain_dot(weights.astype(BF16), g)
        key_grads += plain_dot(score_grads.astype(BF16), q)
    key_grads *= SCALE
    own_ref[:, :HEAD_WIDTH] = key_grads[:half]
    own_ref[:, HEAD_WIDTH:] = value_grads[:half]
    other_ref[:, :HEAD_WIDTH] = key_grads[half:]
    other_ref[:, HEAD_WIDTH:] = value_grads[half:]


def exchanged(value, axes):
    return lax.all_to_all(value, axes, split_axis=0, concat_axis=0, tiled=True)


def shifted(value, axis, by):
    count = lax.axis_size(axis)
    return lax.ppermute(value, axis, [(k, (k + by) % count) for k in range(count)])


def local(
    queries,
    grad_output,
    key_cache,
    saved_value_rows,
    lengths,
    span_index,
    w_query,
    key_projection_weight,
    value_projection_weight,
):
    heads = queries.shape[1] // HEAD_WIDTH
    width = heads * HEAD_WIDTH
    rows = lax.axis_size(FAR)
    block = key_cache.shape[0]
    groups = lax.axis_size("head")
    core = lax.axis_index(CORE)
    far = lax.axis_index(FAR)
    mine = lax.axis_index("head")

    other_length = shifted(lengths, CORE, 1)
    numbers = jnp.stack([lengths // 16, lengths % 16, other_length // 16, other_length % 16], axis=1)
    numbers = jnp.pad(numbers.astype(BF16), ((0, 0), (0, 124)))
    row = jnp.concatenate([queries, grad_output, numbers], axis=1)
    gathered = exchanged(jnp.broadcast_to(row, (rows, 1, row.shape[1])), FAR)
    x = gathered.reshape(rows, row.shape[1])

    cache = jnp.concatenate([key_cache, saved_value_rows], axis=1)
    other_cache = shifted(cache, CORE, 1)
    keys = jnp.concatenate([key_cache, other_cache[:, :HEAD_WIDTH]], axis=0)
    values = jnp.concatenate([saved_value_rows, other_cache[:, HEAD_WIDTH:]], axis=0)

    features = key_projection_weight.shape[0] // groups
    first_is_key = core == 0
    half_weights = jnp.where(first_is_key, key_projection_weight, value_projection_weight)
    half_weights = half_weights.reshape(groups, features, HEAD_WIDTH)
    half_all = exchanged(half_weights, "head")
    other_half = shifted(half_all, CORE, 1)
    key_weights = jnp.where(first_is_key, half_all, other_half)
    value_weights = jnp.where(first_is_key, other_half, half_all)
    joined = jnp.concatenate([key_weights, value_weights], axis=2)

    where = jnp.stack([far, core, span_index[0], jnp.int32(2 * rows)]).astype(jnp.int32)
    y, place = pl.pallas_call(
        functools.partial(first_kernel, heads, min(4, heads)),
        out_shape=(
            jax.ShapeDtypeStruct((rows, 2 * width + 256), BF16),
            jax.ShapeDtypeStruct((4,), F32),
        ),
        in_specs=[SMEM, VMEM, VMEM, VMEM],
        out_specs=(VMEM, SMEM),
        name="row_partials",
    )(where, x, keys, values)
    arrived = exchanged(y.reshape(rows, 1, y.shape[1]), FAR).reshape(y.shape)
    merged = pl.pallas_call(
        functools.partial(merge_kernel, heads),
        out_shape=jax.ShapeDtypeStruct((rows, width + 256), BF16),
        in_specs=[VMEM],
        out_specs=VMEM,
        name="row_merge",
    )(arrived)
    u = exchanged(merged.reshape(rows, 1, merged.shape[1]), FAR).reshape(merged.shape)
    own_part, other_part = pl.pallas_call(
        functools.partial(second_kernel, heads),
        out_shape=(jax.ShapeDtypeStruct((block, 2 * HEAD_WIDTH), F32),) * 2,
        in_specs=[SMEM, SMEM, VMEM, VMEM, VMEM, VMEM],
        out_specs=(VMEM, VMEM),
        name="slot_gradients",
    )(where, place, x, u, keys, values)
    slot_grads = (own_part + shifted(other_part, CORE, 1)).astype(BF16)
    saved_key_gradient = slot_grads[:, :HEAD_WIDTH]
    saved_value_gradient = slot_grads[:, HEAD_WIDTH:]

    pieces = [slot_grads] + [shifted(slot_grads, "head", k) for k in range(1, groups)]
    total = jnp.zeros((block, features), F32)
    for k, piece in enumerate(pieces):
        source = lax.rem(mine - k + groups, groups)
        weights = lax.dynamic_index_in_dim(joined, source, 0, keepdims=False)
        total = total + rows_dot(piece, weights)
    cached_input_gradient = total.astype(BF16)

    query_low = u[:, :width]
    other_low = shifted(query_low, CORE, 1)
    own_rows = rows_dot(query_low, w_query)
    other_rows = rows_dot(other_low, w_query)
    even = jnp.where(first_is_key, own_rows, other_rows)
    odd = jnp.where(first_is_key, other_rows, own_rows)
    span_part = jnp.stack([even, odd], axis=1).reshape(groups, -1, w_query.shape[0])
    grad_span_input = exchanged(span_part, "head").sum(axis=0).astype(BF16)
    return (saved_key_gradient, saved_value_gradient, cached_input_gradient, grad_span_input)


def solution(mesh):
    split = Mesh(
        mesh.devices.reshape(4, 8, 2, 2, mesh.shape["head"]),
        ("seq_0", "seq_1", "seq_2", "seq_3", "head"),
    )
    in_specs = (
        P(SEQ, "head"),
        P(SEQ, "head"),
        P(SEQ, "head"),
        P(SEQ, "head"),
        P(SEQ),
        P(),
        P(SEQ, "head"),
        P(None, "head"),
        P(None, "head"),
    )
    out_specs = (P(SEQ, "head"), P(SEQ, "head"), P(SEQ, "head"), P("head", SEQ))
    return jax.shard_map(local, mesh=split, in_specs=in_specs, out_specs=out_specs, check_vma=False)
```

```python
import functools

import jax
import jax.numpy as jnp
from jax import lax
from jax.experimental import pallas as pl
from jax.experimental.pallas import tpu as pltpu
from jax.sharding import Mesh
from jax.sharding import PartitionSpec as P

HEAD_WIDTH = 128
SEQ = ("seq_0", "seq_1", "seq_2", "seq_3")
FAR = ("seq_0", "seq_1", "seq_2")
CORE = "seq_3"
LOWEST_SCORE = -1e30
LOWEST_PEAK = -1e29
DEAD = 1e9
SCALE = HEAD_WIDTH ** (-0.5)
F32 = jnp.float32
BF16 = jnp.bfloat16
VMEM = pl.BlockSpec(memory_space=pltpu.VMEM)
PARAMS = pltpu.CompilerParams(vmem_limit_bytes=32 * 1024 * 1024)
SMEM = pl.BlockSpec(memory_space=pltpu.SMEM)


def rows_dot(a, b):
    return lax.dot_general(a, b, (((1,), (1,)), ((), ())), preferred_element_type=F32)


def plain_dot(a, b):
    return lax.dot_general(a, b, (((1,), (0,)), ((), ())), preferred_element_type=F32)


def three_parts(value):
    high = value.astype(BF16).astype(F32)
    rest = value - high
    middle = rest.astype(BF16).astype(F32)
    low = (rest - middle).astype(BF16).astype(F32)
    return high, middle, low


def spread(held):
    axis = held.ndim - 1
    high, middle, low = three_parts(held)
    return high + pltpu.roll(middle, 16, axis) + pltpu.roll(low, 32, axis)


def gathered_parts(block):
    wide = block.astype(F32)
    axis = wide.ndim - 1
    return wide + pltpu.roll(wide, 112, axis) + pltpu.roll(wide, 96, axis)


def pack_kernel(heads, own_ref, other_ref, q_ref, g_ref, row_ref):
    lane = lax.broadcasted_iota(jnp.int32, (8, 128), 1)
    own, other = own_ref[0], other_ref[0]
    numbers = jnp.where(lane == 0, own // 16, 0) + jnp.where(lane == 1, own % 16, 0)
    numbers += jnp.where(lane == 2, other // 16, 0) + jnp.where(lane == 3, other % 16, 0)
    lines = []
    for ref in (q_ref, g_ref):
        wide = ref[...].astype(F32)
        lines += [wide[:, h * HEAD_WIDTH : (h + 1) * HEAD_WIDTH] for h in range(heads)]
    row = jnp.concatenate([*lines, numbers.astype(F32)], axis=0).astype(BF16)
    for k in range(row_ref.shape[0]):
        row_ref[k] = row


def first_kernel(heads, group, where_ref, x_ref, k_ref, v_ref, y_ref, place_ref):
    rows = x_ref.shape[0]
    half = k_ref.shape[0] // 2
    far, core, span, row_total = (where_ref[0], where_ref[1], where_ref[2], where_ref[3])
    lens = x_ref[:, 2 * heads :, :].astype(F32)
    lane = lax.broadcasted_iota(jnp.int32, lens.shape, 2)
    row = lax.broadcasted_iota(jnp.int32, lens.shape, 0)
    first_line = lax.broadcasted_iota(jnp.int32, lens.shape, 1) == 0
    lens = lens * jnp.where(first_line & (lane < 4), jnp.where(lane % 2 == 0, 16.0, 1.0), 0.0)
    base = jnp.sum(jnp.where(row < far, lens, 0.0))
    here = jnp.where(row == far, lens, 0.0)
    own = jnp.sum(jnp.where(lane < 2, here, 0.0))
    other = jnp.sum(jnp.where(lane >= 2, here, 0.0))
    is_second = core.astype(F32)
    own_offset = base + is_second * other
    other_offset = base + (1.0 - is_second) * own
    place_ref[0] = own_offset
    place_ref[1] = other_offset
    place_ref[2] = own
    place_ref[3] = other
    within = lax.broadcasted_iota(jnp.int32, (1, half), 1).astype(F32)
    position = jnp.concatenate(
        [
            jnp.where(within < own, own_offset + within, DEAD),
            jnp.where(within < other, other_offset + within, DEAD),
        ],
        axis=1,
    )
    tall = group * heads
    index = lax.broadcasted_iota(jnp.int32, (tall, 1), 0) // heads
    lane = lax.broadcasted_iota(jnp.int32, (tall, 128), 1)
    keys = k_ref[...]
    values = v_ref[...]
    for first in range(0, rows, group):
        part = pl.ds(first, group)
        q = x_ref[part, :heads, :].reshape(tall, HEAD_WIDTH)
        g = x_ref[part, heads : 2 * heads, :].reshape(tall, HEAD_WIDTH)
        asked = (span * row_total + 2 * (first + index) + core).astype(F32)
        scores = jnp.where(position <= asked, rows_dot(q, keys) * SCALE, LOWEST_SCORE)
        peak = jnp.maximum(jnp.max(scores, axis=1, keepdims=True), LOWEST_PEAK)
        raised = jnp.exp(scores - peak)
        grads = rows_dot(g, values)
        total = jnp.sum(raised, axis=1, keepdims=True)
        mean = jnp.sum(raised * grads, axis=1, keepdims=True) / jnp.maximum(total, 0.5)
        moved = (raised * (grads - mean)).astype(BF16)
        both = plain_dot(jnp.concatenate([moved, raised.astype(BF16)], axis=0), keys)
        y_ref[part, :heads, :] = both[:tall].astype(BF16).reshape(group, heads, HEAD_WIDTH)
        y_ref[part, heads : 2 * heads, :] = both[tall:].astype(BF16).reshape(group, heads, HEAD_WIDTH)
        held = jnp.where(lane == 0, peak, jnp.where(lane == 1, total, jnp.where(lane == 2, mean, 0.0)))
        held = spread(held).reshape(group, 2, heads // 2, 128)
        held = held[:, 0] + pltpu.roll(held[:, 1], 64, 2)
        y_ref[part, 2 * heads :, :] = held.astype(BF16)


def merge_kernel(heads, z_ref, u_ref):
    stats = gathered_parts(z_ref[:, 2 * heads :, :])
    total = pltpu.roll(stats, 127, 2)
    mean = pltpu.roll(stats, 126, 2)
    row_peak = jnp.max(stats, axis=0, keepdims=True)
    share = jnp.exp(stats - row_peak)
    part = share * total
    row_total = jnp.sum(part, axis=0, keepdims=True)
    row_mean = jnp.sum(part * mean, axis=0, keepdims=True) / row_total
    moved_factor = share * (SCALE / row_total)
    plain_factor = moved_factor * (mean - row_mean)

    def of_heads(factor):
        return jnp.concatenate([factor[:, :, 0:1], factor[:, :, 64:65]], axis=1)

    term = z_ref[:, :heads, :].astype(F32) * of_heads(moved_factor)
    term += z_ref[:, heads : 2 * heads, :].astype(F32) * of_heads(plain_factor)
    query_grads = jnp.sum(term, axis=0).astype(BF16)
    lane = lax.broadcasted_iota(jnp.int32, (heads // 2, 128), 1) % 64
    found = jnp.where(lane == 0, row_peak[0], 0.0)
    found = jnp.where(lane == 1, pltpu.roll(row_total[0], 1, 1), found)
    found = jnp.where(lane == 2, pltpu.roll(row_mean[0], 2, 1), found)
    found = spread(found).astype(BF16)
    for k in range(u_ref.shape[0]):
        u_ref[k, :heads, :] = query_grads
        u_ref[k, heads:, :] = found


def second_kernel(heads, group, where_ref, place_ref, x_ref, u_ref, k_ref, v_ref, own_ref, other_ref):
    rows = x_ref.shape[0]
    slots = k_ref.shape[0]
    half = slots // 2
    core, span, row_total = (where_ref[1], where_ref[2], where_ref[3])
    within = lax.broadcasted_iota(jnp.int32, (half, 1), 0).astype(F32)
    position = jnp.concatenate(
        [
            jnp.where(within < place_ref[2], place_ref[0] + within, DEAD),
            jnp.where(within < place_ref[3], place_ref[1] + within, DEAD),
        ],
        axis=0,
    )
    wide = group * heads
    index = lax.broadcasted_iota(jnp.int32, (1, wide), 1) // heads
    stats = gathered_parts(u_ref[:, heads:, :])
    keys = k_ref[...]
    values = v_ref[...]
    value_grads = jnp.zeros((slots, HEAD_WIDTH), F32)
    key_grads = jnp.zeros((slots, HEAD_WIDTH), F32)
    for first in range(0, rows, group):
        part = pl.ds(first, group)
        q = x_ref[part, :heads, :].reshape(wide, HEAD_WIDTH)
        g = x_ref[part, heads : 2 * heads, :].reshape(wide, HEAD_WIDTH)
        held = stats[first : first + group]
        held = jnp.concatenate([held, pltpu.roll(held, 64, 2)], axis=1).reshape(wide, 128)
        turned = jnp.transpose(held)
        asked = (span * row_total + 2 * (first + index) + core).astype(F32)
        scores = rows_dot(keys, q) * SCALE
        raised = jnp.exp(jnp.where(position <= asked, scores - turned[0:1], LOWEST_SCORE))
        weights = raised * (1.0 / turned[1:2])
        score_grads = weights * (rows_dot(values, g) - turned[2:3])
        value_grads += plain_dot(weights.astype(BF16), g)
        key_grads += plain_dot(score_grads.astype(BF16), q)
    key_grads *= SCALE
    own_ref[:, :HEAD_WIDTH] = key_grads[:half]
    own_ref[:, HEAD_WIDTH:] = value_grads[:half]
    other_ref[:, :HEAD_WIDTH] = key_grads[half:]
    other_ref[:, HEAD_WIDTH:] = value_grads[half:]


def exchanged(value, axes):
    return lax.all_to_all(value, axes, split_axis=0, concat_axis=0, tiled=True)


def shifted(value, axis, by):
    count = lax.axis_size(axis)
    return lax.ppermute(value, axis, [(k, (k + by) % count) for k in range(count)])


def local(
    queries,
    grad_output,
    key_cache,
    saved_value_rows,
    lengths,
    span_index,
    w_query,
    key_projection_weight,
    value_projection_weight,
):
    heads = queries.shape[1] // HEAD_WIDTH
    rows = lax.axis_size(FAR)
    block = key_cache.shape[0]
    groups = lax.axis_size("head")
    core = lax.axis_index(CORE)
    far = lax.axis_index(FAR)
    mine = lax.axis_index("head")
    lines = 2 * heads + 8
    group = min(16, rows)

    other_length = shifted(lengths, CORE, 1)
    row = pl.pallas_call(
        functools.partial(pack_kernel, heads),
        out_shape=jax.ShapeDtypeStruct((rows, lines, HEAD_WIDTH), BF16),
        in_specs=[SMEM, SMEM, VMEM, VMEM],
        out_specs=VMEM,
        name="row_pack",
        compiler_params=PARAMS,
    )(lengths, other_length, queries, grad_output)
    x = exchanged(row, FAR)

    cache = jnp.concatenate([key_cache, saved_value_rows], axis=1)
    other_cache = shifted(cache, CORE, 1)
    keys = jnp.concatenate([key_cache, other_cache[:, :HEAD_WIDTH]], axis=0)
    values = jnp.concatenate([saved_value_rows, other_cache[:, HEAD_WIDTH:]], axis=0)

    features = key_projection_weight.shape[0] // groups
    first_is_key = core == 0
    half_weights = jnp.where(first_is_key, key_projection_weight, value_projection_weight)
    half_weights = half_weights.reshape(groups, features, HEAD_WIDTH)
    arriving = []
    for k in range(1, groups):
        target = lax.rem(mine + k, groups)
        piece = lax.dynamic_index_in_dim(half_weights, target, 0, keepdims=False)
        arriving.append(shifted(piece, "head", k))
    half_all = jnp.concatenate(arriving, axis=0)
    other_half = shifted(half_all, CORE, 1)
    key_weights = jnp.where(first_is_key, half_all, other_half)
    value_weights = jnp.where(first_is_key, other_half, half_all)
    joined = jnp.concatenate([key_weights, value_weights], axis=1)

    where = jnp.stack([far, core, span_index[0], jnp.int32(2 * rows)]).astype(jnp.int32)
    y, place = pl.pallas_call(
        functools.partial(first_kernel, heads, group),
        out_shape=(
            jax.ShapeDtypeStruct((rows, lines, HEAD_WIDTH), BF16),
            jax.ShapeDtypeStruct((4,), F32),
        ),
        in_specs=[SMEM, VMEM, VMEM, VMEM],
        out_specs=(VMEM, SMEM),
        name="row_partials",
        compiler_params=PARAMS,
    )(where, x, keys, values)
    arrived = exchanged(y, FAR)
    merged = pl.pallas_call(
        functools.partial(merge_kernel, heads),
        out_shape=jax.ShapeDtypeStruct((rows, heads + 8, HEAD_WIDTH), BF16),
        in_specs=[VMEM],
        out_specs=VMEM,
        name="row_merge",
        compiler_params=PARAMS,
    )(arrived)
    u = exchanged(merged, FAR)
    own_part, other_part = pl.pallas_call(
        functools.partial(second_kernel, heads, group),
        out_shape=(jax.ShapeDtypeStruct((block, 2 * HEAD_WIDTH), F32),) * 2,
        in_specs=[SMEM, SMEM, VMEM, VMEM, VMEM, VMEM],
        out_specs=(VMEM, VMEM),
        name="slot_gradients",
        compiler_params=PARAMS,
    )(where, place, x, u, keys, values)
    other_sums = shifted(other_part, CORE, 1)
    slot_grads = (own_part + other_sums).astype(BF16)
    saved_key_gradient = slot_grads[:, :HEAD_WIDTH]
    saved_value_gradient = slot_grads[:, HEAD_WIDTH:]

    pieces = [slot_grads]
    for k in range(1, groups):
        pieces.append(shifted(slot_grads, "head", k))
    own_weights = [
        lax.dynamic_slice_in_dim(w, mine * features, features, 0)
        for w in (key_projection_weight, value_projection_weight)
    ]
    total = rows_dot(slot_grads, jnp.concatenate(own_weights, axis=1))
    for k in range(1, groups):
        total = total + rows_dot(pieces[k], joined[(k - 1) * features : k * features])
    cached_input_gradient = total.astype(BF16)

    query_low = u[:, :heads, :]
    other_low = shifted(query_low, CORE, 1)
    own_rows = rows_dot(query_low.reshape(rows, -1), w_query)
    other_rows = rows_dot(other_low.reshape(rows, -1), w_query)
    even = jnp.where(first_is_key, own_rows, other_rows)
    odd = jnp.where(first_is_key, other_rows, own_rows)
    span_part = jnp.stack([even, odd], axis=1).reshape(groups, -1, w_query.shape[0])
    arrived_parts = exchanged(span_part, "head")
    grad_span_input = arrived_parts.sum(axis=0).astype(BF16)
    return (saved_key_gradient, saved_value_gradient, cached_input_gradient, grad_span_input)


def solution(mesh):
    split = Mesh(
        mesh.devices.reshape(4, 8, 2, 2, mesh.shape["head"]),
        ("seq_0", "seq_1", "seq_2", "seq_3", "head"),
    )
    in_specs = (
        P(SEQ, "head"),
        P(SEQ, "head"),
        P(SEQ, "head"),
        P(SEQ, "head"),
        P(SEQ),
        P(),
        P(SEQ, "head"),
        P(None, "head"),
        P(None, "head"),
    )
    out_specs = (P(SEQ, "head"), P(SEQ, "head"), P(SEQ, "head"), P("head", SEQ))
    return jax.shard_map(local, mesh=split, in_specs=in_specs, out_specs=out_specs, check_vma=False)
```

```python
import functools

import jax
import jax.numpy as jnp
from jax import lax
from jax.experimental import pallas as pl
from jax.experimental.pallas import tpu as pltpu
from jax.sharding import Mesh
from jax.sharding import PartitionSpec as P

HEAD_WIDTH = 128
SEQ = ("seq_0", "seq_1", "seq_2", "seq_3")
FAR = ("seq_0", "seq_1", "seq_2")
CORE = "seq_3"
LOWEST_SCORE = -1e30
LOWEST_PEAK = -1e29
DEAD = 1e9
SCALE = HEAD_WIDTH ** (-0.5)
F32 = jnp.float32
BF16 = jnp.bfloat16
VMEM = pl.BlockSpec(memory_space=pltpu.VMEM)
PARAMS = pltpu.CompilerParams(vmem_limit_bytes=32 * 1024 * 1024)
SMEM = pl.BlockSpec(memory_space=pltpu.SMEM)


def rows_dot(a, b):
    return lax.dot_general(a, b, (((1,), (1,)), ((), ())), preferred_element_type=F32)


def plain_dot(a, b):
    return lax.dot_general(a, b, (((1,), (0,)), ((), ())), preferred_element_type=F32)


def three_parts(value):
    high = value.astype(BF16).astype(F32)
    rest = value - high
    middle = rest.astype(BF16).astype(F32)
    low = (rest - middle).astype(BF16).astype(F32)
    return high, middle, low


def spread(held):
    axis = held.ndim - 1
    high, middle, low = three_parts(held)
    return high + pltpu.roll(middle, 16, axis) + pltpu.roll(low, 32, axis)


def gathered_parts(block):
    wide = block.astype(F32)
    axis = wide.ndim - 1
    return wide + pltpu.roll(wide, 112, axis) + pltpu.roll(wide, 96, axis)


def pack_kernel(heads, own_ref, other_ref, q_ref, g_ref, row_ref):
    lane = lax.broadcasted_iota(jnp.int32, (8, 128), 1)
    own, other = own_ref[0], other_ref[0]
    numbers = jnp.where(lane == 0, own // 16, 0) + jnp.where(lane == 1, own % 16, 0)
    numbers += jnp.where(lane == 2, other // 16, 0) + jnp.where(lane == 3, other % 16, 0)
    lines = []
    for ref in (q_ref, g_ref):
        wide = ref[...].astype(F32)
        lines += [wide[:, h * HEAD_WIDTH : (h + 1) * HEAD_WIDTH] for h in range(heads)]
    row = jnp.concatenate([*lines, numbers.astype(F32)], axis=0).astype(BF16)
    for k in range(row_ref.shape[0]):
        row_ref[k] = row


def first_kernel(heads, group, where_ref, x_ref, k_ref, v_ref, y_ref, place_ref):
    rows = x_ref.shape[0]
    half = k_ref.shape[0] // 2
    far, core, span, row_total = (where_ref[0], where_ref[1], where_ref[2], where_ref[3])
    lens = x_ref[:, 2 * heads :, :].astype(F32)
    lane = lax.broadcasted_iota(jnp.int32, lens.shape, 2)
    row = lax.broadcasted_iota(jnp.int32, lens.shape, 0)
    first_line = lax.broadcasted_iota(jnp.int32, lens.shape, 1) == 0
    lens = lens * jnp.where(first_line & (lane < 4), jnp.where(lane % 2 == 0, 16.0, 1.0), 0.0)
    base = jnp.sum(jnp.where(row < far, lens, 0.0))
    here = jnp.where(row == far, lens, 0.0)
    own = jnp.sum(jnp.where(lane < 2, here, 0.0))
    other = jnp.sum(jnp.where(lane >= 2, here, 0.0))
    is_second = core.astype(F32)
    own_offset = base + is_second * other
    other_offset = base + (1.0 - is_second) * own
    place_ref[0] = own_offset
    place_ref[1] = other_offset
    place_ref[2] = own
    place_ref[3] = other
    within = lax.broadcasted_iota(jnp.int32, (1, half), 1).astype(F32)
    position = jnp.concatenate(
        [
            jnp.where(within < own, own_offset + within, DEAD),
            jnp.where(within < other, other_offset + within, DEAD),
        ],
        axis=1,
    )
    tall = group * heads
    index = lax.broadcasted_iota(jnp.int32, (tall, 1), 0) // heads
    lane = lax.broadcasted_iota(jnp.int32, (tall, 128), 1)
    keys = k_ref[...]
    values = v_ref[...]
    for first in range(0, rows, group):
        part = pl.ds(first, group)
        q = x_ref[part, :heads, :].reshape(tall, HEAD_WIDTH)
        g = x_ref[part, heads : 2 * heads, :].reshape(tall, HEAD_WIDTH)
        asked = (span * row_total + 2 * (first + index) + core).astype(F32)
        scores = jnp.where(position <= asked, rows_dot(q, keys) * SCALE, LOWEST_SCORE)
        peak = jnp.maximum(jnp.max(scores, axis=1, keepdims=True), LOWEST_PEAK)
        raised = jnp.exp(scores - peak)
        grads = rows_dot(g, values)
        total = jnp.sum(raised, axis=1, keepdims=True)
        mean = jnp.sum(raised * grads, axis=1, keepdims=True) / jnp.maximum(total, 0.5)
        moved = (raised * (grads - mean)).astype(BF16)
        both = plain_dot(jnp.concatenate([moved, raised.astype(BF16)], axis=0), keys)
        y_ref[part, :heads, :] = both[:tall].astype(BF16).reshape(group, heads, HEAD_WIDTH)
        y_ref[part, heads : 2 * heads, :] = both[tall:].astype(BF16).reshape(group, heads, HEAD_WIDTH)
        held = jnp.where(lane == 0, peak, jnp.where(lane == 1, total, jnp.where(lane == 2, mean, 0.0)))
        held = spread(held).reshape(group, 2, heads // 2, 128)
        held = held[:, 0] + pltpu.roll(held[:, 1], 64, 2)
        y_ref[part, 2 * heads :, :] = held.astype(BF16)


def merge_kernel(heads, z_ref, u_ref):
    stats = gathered_parts(z_ref[:, 2 * heads :, :])
    total = pltpu.roll(stats, 127, 2)
    mean = pltpu.roll(stats, 126, 2)
    row_peak = jnp.max(stats, axis=0, keepdims=True)
    share = jnp.exp(stats - row_peak)
    part = share * total
    row_total = jnp.sum(part, axis=0, keepdims=True)
    row_mean = jnp.sum(part * mean, axis=0, keepdims=True) / row_total
    moved_factor = share * (SCALE / row_total)
    plain_factor = moved_factor * (mean - row_mean)

    def of_heads(factor):
        return jnp.concatenate([factor[:, :, 0:1], factor[:, :, 64:65]], axis=1)

    term = z_ref[:, :heads, :].astype(F32) * of_heads(moved_factor)
    term += z_ref[:, heads : 2 * heads, :].astype(F32) * of_heads(plain_factor)
    query_grads = jnp.sum(term, axis=0).astype(BF16)
    lane = lax.broadcasted_iota(jnp.int32, (heads // 2, 128), 1) % 64
    found = jnp.where(lane == 0, row_peak[0], 0.0)
    found = jnp.where(lane == 1, pltpu.roll(row_total[0], 1, 1), found)
    found = jnp.where(lane == 2, pltpu.roll(row_mean[0], 2, 1), found)
    found = spread(found).astype(BF16)
    for k in range(u_ref.shape[0]):
        u_ref[k, :heads, :] = query_grads
        u_ref[k, heads:, :] = found


def second_kernel(
    heads, group, where_ref, place_ref, x_ref, u_ref, k_ref, v_ref, w_ref, own_ref, other_ref
):
    rows = x_ref.shape[0]
    slots = k_ref.shape[0]
    half = slots // 2
    core, span, row_total = (where_ref[1], where_ref[2], where_ref[3])
    within = lax.broadcasted_iota(jnp.int32, (half, 1), 0).astype(F32)
    position = jnp.concatenate(
        [
            jnp.where(within < place_ref[2], place_ref[0] + within, DEAD),
            jnp.where(within < place_ref[3], place_ref[1] + within, DEAD),
        ],
        axis=0,
    )
    wide = group * heads
    index = lax.broadcasted_iota(jnp.int32, (1, wide), 1) // heads
    stats = gathered_parts(u_ref[:, heads:, :])
    keys = k_ref[...]
    values = v_ref[...]
    value_grads = jnp.zeros((slots, HEAD_WIDTH), F32)
    key_grads = jnp.zeros((slots, HEAD_WIDTH), F32)
    for first in range(0, rows, group):
        part = pl.ds(first, group)
        q = x_ref[part, :heads, :].reshape(wide, HEAD_WIDTH)
        g = x_ref[part, heads : 2 * heads, :].reshape(wide, HEAD_WIDTH)
        held = stats[first : first + group]
        held = jnp.concatenate([held, pltpu.roll(held, 64, 2)], axis=1).reshape(wide, 128)
        turned = jnp.transpose(held)
        asked = (span * row_total + 2 * (first + index) + core).astype(F32)
        scores = rows_dot(keys, q) * SCALE
        raised = jnp.exp(jnp.where(position <= asked, scores - turned[0:1], LOWEST_SCORE))
        weights = raised * (1.0 / turned[1:2])
        score_grads = weights * (rows_dot(values, g) - turned[2:3])
        value_grads += plain_dot(weights.astype(BF16), g)
        key_grads += plain_dot(score_grads.astype(BF16), q)
    key_grads *= SCALE
    low = jnp.concatenate([u_ref[:, h, :] for h in range(heads)], axis=1)
    features = w_ref.shape[0] // 2
    both = rows_dot(low, w_ref[...])
    for ref, first in ((own_ref, 0), (other_ref, 1)):
        part = slice(first * half, (first + 1) * half)
        ref[:half, :HEAD_WIDTH] = key_grads[part]
        ref[:half, HEAD_WIDTH:] = value_grads[part]
        ref[half:, :] = jnp.zeros((rows, 2 * HEAD_WIDTH), F32)
        ref[half:, :features] = both[:, first * features : (first + 1) * features]


def finish_kernel(groups, features, where_ref, own_ref, other_ref, k_ref, v_ref, span_ref, *out_refs):
    half = k_ref.shape[0]
    per = span_ref.shape[0] // 2
    sums = (own_ref[:half, :] + other_ref[:half, :]).astype(BF16)
    k_ref[...] = sums[:, :HEAD_WIDTH]
    v_ref[...] = sums[:, HEAD_WIDTH:]
    is_first = where_ref[1] == 0
    lane = lax.broadcasted_iota(jnp.int32, (2 * per, 128), 1)

    def block_rows(target):
        start = half + per * target
        if per % 8 == 0:
            start = pl.multiple_of(start, 8)
        part = pl.ds(start, per)
        mine, theirs = own_ref[part, :128], other_ref[part, :128]
        even = jnp.where(is_first, mine, theirs)
        odd = jnp.where(is_first, theirs, mine)
        return jnp.where(lane < features, jnp.concatenate([even, odd], axis=0), 0.0)

    mine = where_ref[4]
    span_ref[...] = block_rows(mine)
    for k, ref in enumerate(out_refs, 1):
        high, middle, low = three_parts(block_rows(lax.rem(mine + k, groups)))
        wide = high + pltpu.roll(middle, features, 1) + pltpu.roll(low, 2 * features, 1)
        ref[:half, :] = sums
        ref[half:, :] = jnp.concatenate([wide, jnp.zeros_like(wide)], axis=1).astype(BF16)


def input_kernel(groups, where_ref, own_ref, span_ref, *refs):
    arrived, refs = refs[: groups - 1], refs[groups - 1 :]
    own_k_ref, own_v_ref = refs[:2]
    here, there = refs[2 : 1 + groups], refs[1 + groups : 2 * groups]
    out_ref, block_ref, turn_ref = refs[2 * groups :]
    half = out_ref.shape[0]
    rows, features = block_ref.shape
    is_first = where_ref[1] == 0
    left = [own_ref[:half, :]]
    span = span_ref[...]
    for ref in arrived:
        keys, values = ref[:half, :HEAD_WIDTH], ref[:half, HEAD_WIDTH:]
        left += [jnp.where(is_first, keys, values), jnp.where(is_first, values, keys)]
        wide = ref[half:, :128].astype(F32)
        span += wide + pltpu.roll(wide, 128 - features, 1) + pltpu.roll(wide, 128 - 2 * features, 1)
    left = jnp.concatenate(left, axis=1)
    step = min(256, out_ref.shape[1])
    for first in range(0, out_ref.shape[1], step):
        part = pl.ds(first, step)
        right = [own_k_ref[part, :], own_v_ref[part, :]]
        for near_ref, far_ref in zip(here, there):
            right += [near_ref[part, :], far_ref[part, :]]
        out_ref[:, part] = rows_dot(left, jnp.concatenate(right, axis=1)).astype(BF16)
    turn_ref[pl.ds(0, rows // 2, stride=2), :] = span[: rows // 2]
    turn_ref[pl.ds(1, rows // 2, stride=2), :] = span[rows // 2 :]
    block_ref[...] = turn_ref[:, :features].astype(BF16)


def exchanged(value, axes):
    return lax.all_to_all(value, axes, split_axis=0, concat_axis=0, tiled=True)


def shifted(value, axis, by):
    count = lax.axis_size(axis)
    return lax.ppermute(value, axis, [(k, (k + by) % count) for k in range(count)])


def local(
    queries,
    grad_output,
    key_cache,
    saved_value_rows,
    lengths,
    span_index,
    w_query,
    key_projection_weight,
    value_projection_weight,
):
    heads = queries.shape[1] // HEAD_WIDTH
    rows = lax.axis_size(FAR)
    block = key_cache.shape[0]
    groups = lax.axis_size("head")
    core = lax.axis_index(CORE)
    far = lax.axis_index(FAR)
    mine = lax.axis_index("head")
    lines = 2 * heads + 8
    group = min(16, rows)

    other_length = shifted(lengths, CORE, 1)
    row = pl.pallas_call(
        functools.partial(pack_kernel, heads),
        out_shape=jax.ShapeDtypeStruct((rows, lines, HEAD_WIDTH), BF16),
        in_specs=[SMEM, SMEM, VMEM, VMEM],
        out_specs=VMEM,
        name="row_pack",
    )(lengths, other_length, queries, grad_output)
    x = exchanged(row, FAR)

    cache = jnp.concatenate([key_cache, saved_value_rows], axis=1)
    other_cache = shifted(cache, CORE, 1)
    keys = jnp.concatenate([key_cache, other_cache[:, :HEAD_WIDTH]], axis=0)
    values = jnp.concatenate([saved_value_rows, other_cache[:, HEAD_WIDTH:]], axis=0)

    features = key_projection_weight.shape[0] // groups
    first_is_key = core == 0
    half_weights = jnp.where(first_is_key, key_projection_weight, value_projection_weight)
    half_weights = half_weights.reshape(groups, features, HEAD_WIDTH)
    arriving = []
    for k in range(1, groups):
        target = lax.rem(mine + k, groups)
        piece = lax.dynamic_index_in_dim(half_weights, target, 0, keepdims=False)
        arriving.append(shifted(piece, "head", k))
    other_half = []
    for k, piece in enumerate(arriving, 1):
        other_half.append(shifted(piece, CORE, 1))
    own_weights = [
        lax.dynamic_slice_in_dim(w, mine * features, features, 0)
        for w in (key_projection_weight, value_projection_weight)
    ]
    other_query = shifted(w_query, CORE, 1)
    both_query = jnp.concatenate([w_query, other_query], axis=0)

    where = jnp.full((8,), 2 * rows, jnp.int32)
    for k, number in ((0, far), (1, core), (2, span_index[0]), (4, mine)):
        where = jnp.where(jnp.arange(8) == k, number, where)
    y, place = pl.pallas_call(
        functools.partial(first_kernel, heads, group),
        out_shape=(
            jax.ShapeDtypeStruct((rows, lines, HEAD_WIDTH), BF16),
            jax.ShapeDtypeStruct((4,), F32),
        ),
        in_specs=[SMEM, VMEM, VMEM, VMEM],
        out_specs=(VMEM, SMEM),
        name="row_partials",
        compiler_params=PARAMS,
    )(where, x, keys, values)
    arrived = exchanged(y, FAR)
    merged = pl.pallas_call(
        functools.partial(merge_kernel, heads),
        out_shape=jax.ShapeDtypeStruct((rows, heads + 8, HEAD_WIDTH), BF16),
        in_specs=[VMEM],
        out_specs=VMEM,
        name="row_merge",
        compiler_params=PARAMS,
    )(arrived)
    u = exchanged(merged, FAR)
    width = w_query.shape[0]
    own_part, other_part = pl.pallas_call(
        functools.partial(second_kernel, heads, group),
        out_shape=(jax.ShapeDtypeStruct((block + rows, 2 * HEAD_WIDTH), F32),) * 2,
        in_specs=[SMEM, SMEM, VMEM, VMEM, VMEM, VMEM, VMEM],
        out_specs=(VMEM, VMEM),
        name="slot_gradients",
        compiler_params=PARAMS,
    )(where, place, x, u, keys, values, both_query)
    other_sums = shifted(other_part, CORE, 1)
    per = rows // groups
    saved_key_gradient, saved_value_gradient, own_span, *leaving = pl.pallas_call(
        functools.partial(finish_kernel, groups, width),
        out_shape=(
            jax.ShapeDtypeStruct((block, HEAD_WIDTH), BF16),
            jax.ShapeDtypeStruct((block, HEAD_WIDTH), BF16),
            jax.ShapeDtypeStruct((2 * per, 128), F32),
        )
        + (jax.ShapeDtypeStruct((block + 2 * per, 2 * HEAD_WIDTH), BF16),) * (groups - 1),
        in_specs=[SMEM, VMEM, VMEM],
        out_specs=(VMEM,) * (2 + groups),
        name="slot_sums",
        compiler_params=PARAMS,
    )(where, own_part, other_sums)

    pieces = []
    for k, piece in enumerate(leaving, 1):
        pieces.append(shifted(piece, "head", k))
    cached_input_gradient, grad_span_input = pl.pallas_call(
        functools.partial(input_kernel, groups),
        out_shape=(
            jax.ShapeDtypeStruct((block, features), BF16),
            jax.ShapeDtypeStruct((2 * per, width), BF16),
        ),
        in_specs=[SMEM] + [VMEM] * (1 + 3 * groups),
        out_specs=(VMEM, VMEM),
        scratch_shapes=[pltpu.VMEM((2 * per, 128), F32)],
        name="input_gradient",
        compiler_params=PARAMS,
    )(
        where,
        leaving[0],
        own_span,
        *pieces,
        *own_weights,
        *arriving,
        *other_half,
    )
    return (saved_key_gradient, saved_value_gradient, cached_input_gradient, grad_span_input)


def solution(mesh):
    split = Mesh(
        mesh.devices.reshape(4, 8, 2, 2, mesh.shape["head"]),
        ("seq_0", "seq_1", "seq_2", "seq_3", "head"),
    )
    in_specs = (
        P(SEQ, "head"),
        P(SEQ, "head"),
        P(SEQ, "head"),
        P(SEQ, "head"),
        P(SEQ),
        P(),
        P(SEQ, "head"),
        P(None, "head"),
        P(None, "head"),
    )
    out_specs = (P(SEQ, "head"), P(SEQ, "head"), P(SEQ, "head"), P("head", SEQ))
    return jax.shard_map(local, mesh=split, in_specs=in_specs, out_specs=out_specs, check_vma=False)
```

```python
import functools

import jax
import jax.numpy as jnp
from jax import lax
from jax.experimental import pallas as pl
from jax.experimental.pallas import tpu as pltpu
from jax.sharding import Mesh
from jax.sharding import PartitionSpec as P

HEAD_WIDTH = 128
SEQ = ("seq_0", "seq_1", "seq_2", "seq_3")
FAR = ("seq_0", "seq_1", "seq_2")
CORE = "seq_3"
LOWEST_SCORE = -1e30
LOWEST_PEAK = -1e29
DEAD = 1e9
SCALE = HEAD_WIDTH ** (-0.5)
F32 = jnp.float32
BF16 = jnp.bfloat16
VMEM = pl.BlockSpec(memory_space=pltpu.VMEM)
PARAMS = pltpu.CompilerParams(vmem_limit_bytes=32 * 1024 * 1024)
SMEM = pl.BlockSpec(memory_space=pltpu.SMEM)


def rows_dot(a, b):
    return lax.dot_general(a, b, (((1,), (1,)), ((), ())), preferred_element_type=F32)


def plain_dot(a, b):
    return lax.dot_general(a, b, (((1,), (0,)), ((), ())), preferred_element_type=F32)


def three_parts(value):
    high = value.astype(BF16).astype(F32)
    rest = value - high
    middle = rest.astype(BF16).astype(F32)
    low = (rest - middle).astype(BF16).astype(F32)
    return high, middle, low


def spread(held):
    axis = held.ndim - 1
    high, middle, low = three_parts(held)
    return high + pltpu.roll(middle, 16, axis) + pltpu.roll(low, 32, axis)


def gathered_parts(block):
    wide = block.astype(F32)
    axis = wide.ndim - 1
    return wide + pltpu.roll(wide, 112, axis) + pltpu.roll(wide, 96, axis)


def pack_kernel(heads, own_ref, other_ref, q_ref, g_ref, row_ref):
    lane = lax.broadcasted_iota(jnp.int32, (8, 128), 1)
    own, other = own_ref[0], other_ref[0]
    numbers = jnp.where(lane == 0, own // 16, 0) + jnp.where(lane == 1, own % 16, 0)
    numbers += jnp.where(lane == 2, other // 16, 0) + jnp.where(lane == 3, other % 16, 0)
    lines = []
    for ref in (q_ref, g_ref):
        wide = ref[...].astype(F32)
        lines += [wide[:, h * HEAD_WIDTH : (h + 1) * HEAD_WIDTH] for h in range(heads)]
    row = jnp.concatenate([*lines, numbers.astype(F32)], axis=0).astype(BF16)
    for k in range(row_ref.shape[0]):
        row_ref[k] = row


def first_kernel(heads, group, where_ref, x_ref, k_ref, v_ref, y_ref, place_ref):
    rows = x_ref.shape[0]
    half = k_ref.shape[0] // 2
    far, core, span, row_total = (where_ref[0], where_ref[1], where_ref[2], where_ref[3])
    lens = x_ref[:, 2 * heads :, :].astype(F32)
    lane = lax.broadcasted_iota(jnp.int32, lens.shape, 2)
    row = lax.broadcasted_iota(jnp.int32, lens.shape, 0)
    first_line = lax.broadcasted_iota(jnp.int32, lens.shape, 1) == 0
    lens = lens * jnp.where(first_line & (lane < 4), jnp.where(lane % 2 == 0, 16.0, 1.0), 0.0)
    base = jnp.sum(jnp.where(row < far, lens, 0.0))
    here = jnp.where(row == far, lens, 0.0)
    own = jnp.sum(jnp.where(lane < 2, here, 0.0))
    other = jnp.sum(jnp.where(lane >= 2, here, 0.0))
    is_second = core.astype(F32)
    own_offset = base + is_second * other
    other_offset = base + (1.0 - is_second) * own
    place_ref[0] = own_offset
    place_ref[1] = other_offset
    place_ref[2] = own
    place_ref[3] = other
    within = lax.broadcasted_iota(jnp.int32, (1, half), 1).astype(F32)
    position = jnp.concatenate(
        [
            jnp.where(within < own, own_offset + within, DEAD),
            jnp.where(within < other, other_offset + within, DEAD),
        ],
        axis=1,
    )
    tall = group * heads
    index = lax.broadcasted_iota(jnp.int32, (tall, 1), 0) // heads
    lane = lax.broadcasted_iota(jnp.int32, (tall, 128), 1)
    keys = k_ref[...]
    values = v_ref[...]
    for first in range(0, rows, group):
        part = pl.ds(first, group)
        q = x_ref[part, :heads, :].reshape(tall, HEAD_WIDTH)
        g = x_ref[part, heads : 2 * heads, :].reshape(tall, HEAD_WIDTH)
        asked = (span * row_total + 2 * (first + index) + core).astype(F32)
        scores = jnp.where(position <= asked, rows_dot(q, keys) * SCALE, LOWEST_SCORE)
        peak = jnp.maximum(jnp.max(scores, axis=1, keepdims=True), LOWEST_PEAK)
        raised = jnp.exp(scores - peak)
        grads = rows_dot(g, values)
        total = jnp.sum(raised, axis=1, keepdims=True)
        mean = jnp.sum(raised * grads, axis=1, keepdims=True) / jnp.maximum(total, 0.5)
        moved = (raised * (grads - mean)).astype(BF16)
        both = plain_dot(jnp.concatenate([moved, raised.astype(BF16)], axis=0), keys)
        y_ref[part, :heads, :] = both[:tall].astype(BF16).reshape(group, heads, HEAD_WIDTH)
        y_ref[part, heads : 2 * heads, :] = both[tall:].astype(BF16).reshape(group, heads, HEAD_WIDTH)
        held = jnp.where(lane == 0, peak, jnp.where(lane == 1, total, jnp.where(lane == 2, mean, 0.0)))
        held = spread(held).reshape(group, 2, heads // 2, 128)
        held = held[:, 0] + pltpu.roll(held[:, 1], 64, 2)
        y_ref[part, 2 * heads :, :] = held.astype(BF16)


def merge_kernel(heads, z_ref, u_ref):
    stats = gathered_parts(z_ref[:, 2 * heads :, :])
    total = pltpu.roll(stats, 127, 2)
    mean = pltpu.roll(stats, 126, 2)
    row_peak = jnp.max(stats, axis=0, keepdims=True)
    share = jnp.exp(stats - row_peak)
    part = share * total
    row_total = jnp.sum(part, axis=0, keepdims=True)
    row_mean = jnp.sum(part * mean, axis=0, keepdims=True) / row_total
    moved_factor = share * (SCALE / row_total)
    plain_factor = moved_factor * (mean - row_mean)

    def of_heads(factor):
        return jnp.concatenate([factor[:, :, 0:1], factor[:, :, 64:65]], axis=1)

    term = z_ref[:, :heads, :].astype(F32) * of_heads(moved_factor)
    term += z_ref[:, heads : 2 * heads, :].astype(F32) * of_heads(plain_factor)
    query_grads = jnp.sum(term, axis=0).astype(BF16)
    lane = lax.broadcasted_iota(jnp.int32, (heads // 2, 128), 1) % 64
    found = jnp.where(lane == 0, row_peak[0], 0.0)
    found = jnp.where(lane == 1, pltpu.roll(row_total[0], 1, 1), found)
    found = jnp.where(lane == 2, pltpu.roll(row_mean[0], 2, 1), found)
    found = spread(found).astype(BF16)
    for k in range(u_ref.shape[0]):
        u_ref[k, :heads, :] = query_grads
        u_ref[k, heads:, :] = found


def second_kernel(
    heads, group, where_ref, place_ref, x_ref, u_ref, k_ref, v_ref, w_ref, own_ref, other_ref
):
    rows = x_ref.shape[0]
    slots = k_ref.shape[0]
    half = slots // 2
    core, span, row_total = (where_ref[1], where_ref[2], where_ref[3])
    within = lax.broadcasted_iota(jnp.int32, (half, 1), 0).astype(F32)
    position = jnp.concatenate(
        [
            jnp.where(within < place_ref[2], place_ref[0] + within, DEAD),
            jnp.where(within < place_ref[3], place_ref[1] + within, DEAD),
        ],
        axis=0,
    )
    wide = group * heads
    index = lax.broadcasted_iota(jnp.int32, (1, wide), 1) // heads
    stats = gathered_parts(u_ref[:, heads:, :])
    keys = k_ref[...]
    values = v_ref[...]
    value_grads = jnp.zeros((slots, HEAD_WIDTH), F32)
    key_grads = jnp.zeros((slots, HEAD_WIDTH), F32)
    for first in range(0, rows, group):
        part = pl.ds(first, group)
        q = x_ref[part, :heads, :].reshape(wide, HEAD_WIDTH)
        g = x_ref[part, heads : 2 * heads, :].reshape(wide, HEAD_WIDTH)
        held = stats[first : first + group]
        held = jnp.concatenate([held, pltpu.roll(held, 64, 2)], axis=1).reshape(wide, 128)
        turned = jnp.transpose(held)
        asked = (span * row_total + 2 * (first + index) + core).astype(F32)
        scores = rows_dot(keys, q) * SCALE
        raised = jnp.exp(jnp.where(position <= asked, scores - turned[0:1], LOWEST_SCORE))
        weights = raised * (1.0 / turned[1:2])
        score_grads = weights * (rows_dot(values, g) - turned[2:3])
        value_grads += plain_dot(weights.astype(BF16), g)
        key_grads += plain_dot(score_grads.astype(BF16), q)
    key_grads *= SCALE
    low = jnp.concatenate([u_ref[:, h, :] for h in range(heads)], axis=1)
    features = w_ref.shape[0] // 2
    both = rows_dot(low, w_ref[...])
    for ref, first in ((own_ref, 0), (other_ref, 1)):
        part = slice(first * half, (first + 1) * half)
        ref[:half, :HEAD_WIDTH] = key_grads[part]
        ref[:half, HEAD_WIDTH:] = value_grads[part]
        ref[half:, :] = jnp.zeros((rows, 2 * HEAD_WIDTH), F32)
        ref[half:, :features] = both[:, first * features : (first + 1) * features]


def finish_kernel(groups, features, where_ref, own_ref, other_ref, k_ref, v_ref, span_ref, *out_refs):
    half = k_ref.shape[0]
    per = span_ref.shape[0] // 2
    sums = (own_ref[:half, :] + other_ref[:half, :]).astype(BF16)
    k_ref[...] = sums[:, :HEAD_WIDTH]
    v_ref[...] = sums[:, HEAD_WIDTH:]
    is_first = where_ref[1] == 0
    lane = lax.broadcasted_iota(jnp.int32, (2 * per, 128), 1)

    def block_rows(target):
        start = half + per * target
        if per % 8 == 0:
            start = pl.multiple_of(start, 8)
        part = pl.ds(start, per)
        mine, theirs = own_ref[part, :128], other_ref[part, :128]
        even = jnp.where(is_first, mine, theirs)
        odd = jnp.where(is_first, theirs, mine)
        return jnp.where(lane < features, jnp.concatenate([even, odd], axis=0), 0.0)

    mine = where_ref[4]
    span_ref[...] = block_rows(mine)

    def share_of(target):
        high, middle, low = three_parts(block_rows(target))
        wide = high + pltpu.roll(middle, features, 1) + pltpu.roll(low, 2 * features, 1)
        return jnp.concatenate([wide, jnp.zeros_like(wide)], axis=1).astype(BF16)

    cut = half // 2
    upper, lower = sums[:cut], sums[cut:]
    relayed_ref, back_ref, ahead_ref, behind_ref = out_refs
    relayed_ref[:cut, :] = upper
    relayed_ref[cut:, :] = share_of(lax.rem(mine + 2, groups))
    back_ref[...] = lower
    ahead_ref[:cut, :] = lower
    ahead_ref[cut:, :] = share_of(lax.rem(mine + 1, groups))
    behind_ref[:cut, :] = upper
    behind_ref[cut:, :] = share_of(lax.rem(mine + 3, groups))


def input_kernel(groups, sharers, where_ref, *refs):
    own_upper_ref, own_lower_ref, span_ref = refs[:3]
    arrived = (refs[3:5], refs[5:7], refs[7:9])
    own_k_ref, own_v_ref = refs[9:11]
    here, there = refs[11 : 11 + sharers], refs[11 + sharers : 11 + 2 * sharers]
    out_ref, block_ref, turn_ref = refs[11 + 2 * sharers :]
    cut = out_ref.shape[0] // 2
    rows, features = block_ref.shape
    is_first = where_ref[1] == 0
    left = [jnp.concatenate([own_upper_ref[:cut, :], own_lower_ref[:cut, :]], axis=0)]
    span = span_ref[...]
    for upper_ref, lower_ref in arrived:
        both = jnp.concatenate([upper_ref[:cut, :], lower_ref[:cut, :]], axis=0)
        keys, values = both[:, :HEAD_WIDTH], both[:, HEAD_WIDTH:]
        left += [jnp.where(is_first, keys, values), jnp.where(is_first, values, keys)]
    for ref in (arrived[0][1], arrived[1][0], arrived[2][0]):
        wide = ref[cut:, :128].astype(F32)
        span += wide + pltpu.roll(wide, 128 - features, 1) + pltpu.roll(wide, 128 - 2 * features, 1)
    left = jnp.concatenate(left, axis=1)
    share = out_ref.shape[1] // sharers
    for k, (near_ref, far_ref) in enumerate(zip(here, there)):
        first = lax.rem(where_ref[5] - k + sharers, sharers) * share
        part = pl.ds(pl.multiple_of(first, share), share)
        right = [own_k_ref[part, :], own_v_ref[part, :]]
        for other in range(groups - 1):
            right += [ref[other * share : (other + 1) * share, :] for ref in (near_ref, far_ref)]
        out_ref[:, part] = rows_dot(left, jnp.concatenate(right, axis=1)).astype(BF16)
    turn_ref[pl.ds(0, rows // 2, stride=2), :] = span[: rows // 2]
    turn_ref[pl.ds(1, rows // 2, stride=2), :] = span[rows // 2 :]
    block_ref[...] = turn_ref[:, :features].astype(BF16)


def exchanged(value, axes):
    return lax.all_to_all(value, axes, split_axis=0, concat_axis=0, tiled=True)


def shifted(value, axis, by):
    count = lax.axis_size(axis)
    return lax.ppermute(value, axis, [(k, (k + by) % count) for k in range(count)])


def local(
    queries,
    grad_output,
    key_cache,
    saved_value_rows,
    lengths,
    span_index,
    w_query,
    key_projection_weight,
    value_projection_weight,
):
    heads = queries.shape[1] // HEAD_WIDTH
    rows = lax.axis_size(FAR)
    block = key_cache.shape[0]
    groups = lax.axis_size("head")
    core = lax.axis_index(CORE)
    far = lax.axis_index(FAR)
    mine = lax.axis_index("head")
    lines = 2 * heads + 8
    group = min(16, rows)

    other_length = shifted(lengths, CORE, 1)
    row = pl.pallas_call(
        functools.partial(pack_kernel, heads),
        out_shape=jax.ShapeDtypeStruct((rows, lines, HEAD_WIDTH), BF16),
        in_specs=[SMEM, SMEM, VMEM, VMEM],
        out_specs=VMEM,
        name="row_pack",
    )(lengths, other_length, queries, grad_output)
    x = exchanged(row, FAR)

    cache = jnp.concatenate([key_cache, saved_value_rows], axis=1)
    other_cache = shifted(cache, CORE, 1)
    keys = jnp.concatenate([key_cache, other_cache[:, :HEAD_WIDTH]], axis=0)
    values = jnp.concatenate([saved_value_rows, other_cache[:, HEAD_WIDTH:]], axis=0)

    features = key_projection_weight.shape[0] // groups
    sharers = lax.axis_size("seq_0")
    share = features // sharers
    first_is_key = core == 0
    half_weights = jnp.where(first_is_key, key_projection_weight, value_projection_weight)
    arriving = []
    for k in range(1, groups):
        start = lax.rem(mine + k, groups) * features + lax.axis_index("seq_0") * share
        piece = lax.dynamic_slice_in_dim(half_weights, start, share, 0)
        arriving.append(shifted(piece, "head", k))
    near = [jnp.concatenate(arriving, axis=0)]
    for k in range(1, sharers):
        near.append(shifted(near[0], "seq_0", k))
    there = []
    for piece in near:
        there.append(shifted(piece, CORE, 1))
    own_weights = [
        lax.dynamic_slice_in_dim(w, mine * features, features, 0)
        for w in (key_projection_weight, value_projection_weight)
    ]
    other_query = shifted(w_query, CORE, 1)
    both_query = jnp.concatenate([w_query, other_query], axis=0)

    where = jnp.full((8,), 2 * rows, jnp.int32)
    for k, number in ((0, far), (1, core), (2, span_index[0]), (4, mine), (5, lax.axis_index("seq_0"))):
        where = jnp.where(jnp.arange(8) == k, number, where)
    y, place = pl.pallas_call(
        functools.partial(first_kernel, heads, group),
        out_shape=(
            jax.ShapeDtypeStruct((rows, lines, HEAD_WIDTH), BF16),
            jax.ShapeDtypeStruct((4,), F32),
        ),
        in_specs=[SMEM, VMEM, VMEM, VMEM],
        out_specs=(VMEM, SMEM),
        name="row_partials",
        compiler_params=PARAMS,
    )(where, x, keys, values)
    arrived = exchanged(y, FAR)
    merged = pl.pallas_call(
        functools.partial(merge_kernel, heads),
        out_shape=jax.ShapeDtypeStruct((rows, heads + 8, HEAD_WIDTH), BF16),
        in_specs=[VMEM],
        out_specs=VMEM,
        name="row_merge",
        compiler_params=PARAMS,
    )(arrived)
    u = exchanged(merged, FAR)
    width = w_query.shape[0]
    own_part, other_part = pl.pallas_call(
        functools.partial(second_kernel, heads, group),
        out_shape=(jax.ShapeDtypeStruct((block + rows, 2 * HEAD_WIDTH), F32),) * 2,
        in_specs=[SMEM, SMEM, VMEM, VMEM, VMEM, VMEM, VMEM],
        out_specs=(VMEM, VMEM),
        name="slot_gradients",
        compiler_params=PARAMS,
    )(where, place, x, u, keys, values, both_query)
    other_sums = shifted(other_part, CORE, 1)
    per = rows // groups
    saved_key_gradient, saved_value_gradient, own_span, *leaving = pl.pallas_call(
        functools.partial(finish_kernel, groups, width),
        out_shape=(
            jax.ShapeDtypeStruct((block, HEAD_WIDTH), BF16),
            jax.ShapeDtypeStruct((block, HEAD_WIDTH), BF16),
            jax.ShapeDtypeStruct((2 * per, 128), F32),
        )
        + tuple(
            jax.ShapeDtypeStruct((block // 2 + more, 2 * HEAD_WIDTH), BF16)
            for more in (2 * per, 0, 2 * per, 2 * per)
        ),
        in_specs=[SMEM, VMEM, VMEM],
        out_specs=(VMEM,) * 7,
        name="slot_sums",
        compiler_params=PARAMS,
    )(where, own_part, other_sums)

    relayed, back, ahead, behind = leaving
    upper_1 = shifted(relayed, "head", 1)
    lower_3 = shifted(back, "head", -1)
    lower_1 = shifted(ahead, "head", 1)
    upper_3 = shifted(behind, "head", -1)
    upper_2 = shifted(upper_1, "head", 1)
    lower_2 = shifted(lower_3, "head", -1)
    cached_input_gradient, grad_span_input = pl.pallas_call(
        functools.partial(input_kernel, groups, sharers),
        out_shape=(
            jax.ShapeDtypeStruct((block, features), BF16),
            jax.ShapeDtypeStruct((2 * per, width), BF16),
        ),
        in_specs=[SMEM] + [VMEM] * (11 + 2 * sharers),
        out_specs=(VMEM, VMEM),
        scratch_shapes=[pltpu.VMEM((2 * per, 128), F32)],
        name="input_gradient",
        compiler_params=PARAMS,
    )(
        where,
        relayed,
        back,
        own_span,
        upper_1,
        lower_1,
        upper_2,
        lower_2,
        upper_3,
        lower_3,
        *own_weights,
        *near,
        *there,
    )
    return (saved_key_gradient, saved_value_gradient, cached_input_gradient, grad_span_input)


def solution(mesh):
    split = Mesh(
        mesh.devices.reshape(4, 8, 2, 2, mesh.shape["head"]),
        ("seq_0", "seq_1", "seq_2", "seq_3", "head"),
    )
    in_specs = (
        P(SEQ, "head"),
        P(SEQ, "head"),
        P(SEQ, "head"),
        P(SEQ, "head"),
        P(SEQ),
        P(),
        P(SEQ, "head"),
        P(None, "head"),
        P(None, "head"),
    )
    out_specs = (P(SEQ, "head"), P(SEQ, "head"), P(SEQ, "head"), P("head", SEQ))
    return jax.shard_map(local, mesh=split, in_specs=in_specs, out_specs=out_specs, check_vma=False)
```

```python
import functools

import jax
import jax.numpy as jnp
from jax import lax
from jax.experimental import pallas as pl
from jax.experimental.pallas import tpu as pltpu
from jax.sharding import Mesh
from jax.sharding import PartitionSpec as P

HEAD_WIDTH = 128
SEQ = ("seq_0", "seq_1", "seq_2", "seq_3")
FAR = ("seq_0", "seq_1", "seq_2")
CORE = "seq_3"
LOWEST_SCORE = -1e30
LOWEST_PEAK = -1e29
DEAD = 1e9
SCALE = HEAD_WIDTH ** (-0.5)
F32 = jnp.float32
BF16 = jnp.bfloat16
VMEM = pl.BlockSpec(memory_space=pltpu.VMEM)
PARAMS = pltpu.CompilerParams(vmem_limit_bytes=32 * 1024 * 1024)
SMEM = pl.BlockSpec(memory_space=pltpu.SMEM)


def rows_dot(a, b):
    return lax.dot_general(a, b, (((1,), (1,)), ((), ())), preferred_element_type=F32)


def plain_dot(a, b):
    return lax.dot_general(a, b, (((1,), (0,)), ((), ())), preferred_element_type=F32)


def three_parts(value):
    high = value.astype(BF16).astype(F32)
    rest = value - high
    middle = rest.astype(BF16).astype(F32)
    low = (rest - middle).astype(BF16).astype(F32)
    return high, middle, low


def spread(held):
    axis = held.ndim - 1
    high, middle, low = three_parts(held)
    return high + pltpu.roll(middle, 16, axis) + pltpu.roll(low, 32, axis)


def gathered_parts(block):
    wide = block.astype(F32)
    axis = wide.ndim - 1
    return wide + pltpu.roll(wide, 112, axis) + pltpu.roll(wide, 96, axis)


def pack_kernel(heads, own_ref, other_ref, q_ref, g_ref, row_ref):
    lane = lax.broadcasted_iota(jnp.int32, (8, 128), 1)
    own, other = own_ref[0], other_ref[0]
    numbers = jnp.where(lane == 0, own // 16, 0) + jnp.where(lane == 1, own % 16, 0)
    numbers += jnp.where(lane == 2, other // 16, 0) + jnp.where(lane == 3, other % 16, 0)
    lines = []
    for ref in (q_ref, g_ref):
        wide = ref[...].astype(F32)
        lines += [wide[:, h * HEAD_WIDTH : (h + 1) * HEAD_WIDTH] for h in range(heads)]
    row = jnp.concatenate([*lines, numbers.astype(F32)], axis=0).astype(BF16)
    for k in range(row_ref.shape[0]):
        row_ref[k] = row


def first_kernel(heads, group, where_ref, x_ref, k_ref, v_ref, y_ref, place_ref):
    rows = x_ref.shape[0]
    half = k_ref.shape[0] // 2
    far, core, span, row_total = (where_ref[0], where_ref[1], where_ref[2], where_ref[3])
    lens = x_ref[:, 2 * heads :, :].astype(F32)
    lane = lax.broadcasted_iota(jnp.int32, lens.shape, 2)
    row = lax.broadcasted_iota(jnp.int32, lens.shape, 0)
    first_line = lax.broadcasted_iota(jnp.int32, lens.shape, 1) == 0
    lens = lens * jnp.where(first_line & (lane < 4), jnp.where(lane % 2 == 0, 16.0, 1.0), 0.0)
    base = jnp.sum(jnp.where(row < far, lens, 0.0))
    here = jnp.where(row == far, lens, 0.0)
    own = jnp.sum(jnp.where(lane < 2, here, 0.0))
    other = jnp.sum(jnp.where(lane >= 2, here, 0.0))
    is_second = core.astype(F32)
    own_offset = base + is_second * other
    other_offset = base + (1.0 - is_second) * own
    place_ref[0] = own_offset
    place_ref[1] = other_offset
    place_ref[2] = own
    place_ref[3] = other
    within = lax.broadcasted_iota(jnp.int32, (1, half), 1).astype(F32)
    position = jnp.concatenate(
        [
            jnp.where(within < own, own_offset + within, DEAD),
            jnp.where(within < other, other_offset + within, DEAD),
        ],
        axis=1,
    )
    tall = group * heads
    index = lax.broadcasted_iota(jnp.int32, (tall, 1), 0) // heads
    lane = lax.broadcasted_iota(jnp.int32, (tall, 128), 1)
    keys = k_ref[...]
    values = v_ref[...]
    for first in range(0, rows, group):
        part = pl.ds(first, group)
        q = x_ref[part, :heads, :].reshape(tall, HEAD_WIDTH)
        g = x_ref[part, heads : 2 * heads, :].reshape(tall, HEAD_WIDTH)
        asked = (span * row_total + 2 * (first + index) + core).astype(F32)
        scores = jnp.where(position <= asked, rows_dot(q, keys) * SCALE, LOWEST_SCORE)
        peak = jnp.maximum(jnp.max(scores, axis=1, keepdims=True), LOWEST_PEAK)
        raised = jnp.exp(scores - peak)
        grads = rows_dot(g, values)
        total = jnp.sum(raised, axis=1, keepdims=True)
        mean = jnp.sum(raised * grads, axis=1, keepdims=True) / jnp.maximum(total, 0.5)
        moved = (raised * (grads - mean)).astype(BF16)
        both = plain_dot(jnp.concatenate([moved, raised.astype(BF16)], axis=0), keys)
        y_ref[part, :heads, :] = both[:tall].astype(BF16).reshape(group, heads, HEAD_WIDTH)
        y_ref[part, heads : 2 * heads, :] = both[tall:].astype(BF16).reshape(group, heads, HEAD_WIDTH)
        held = jnp.where(lane == 0, peak, jnp.where(lane == 1, total, jnp.where(lane == 2, mean, 0.0)))
        held = spread(held).reshape(group, 2, heads // 2, 128)
        held = held[:, 0] + pltpu.roll(held[:, 1], 64, 2)
        y_ref[part, 2 * heads :, :] = held.astype(BF16)


def merge_kernel(heads, z_ref, u_ref):
    stats = gathered_parts(z_ref[:, 2 * heads :, :])
    total = pltpu.roll(stats, 127, 2)
    mean = pltpu.roll(stats, 126, 2)
    row_peak = jnp.max(stats, axis=0, keepdims=True)
    share = jnp.exp(stats - row_peak)
    part = share * total
    row_total = jnp.sum(part, axis=0, keepdims=True)
    row_mean = jnp.sum(part * mean, axis=0, keepdims=True) / row_total
    moved_factor = share * (SCALE / row_total)
    plain_factor = moved_factor * (mean - row_mean)

    def of_heads(factor):
        return jnp.concatenate([factor[:, :, 0:1], factor[:, :, 64:65]], axis=1)

    term = z_ref[:, :heads, :].astype(F32) * of_heads(moved_factor)
    term += z_ref[:, heads : 2 * heads, :].astype(F32) * of_heads(plain_factor)
    query_grads = jnp.sum(term, axis=0).astype(BF16)
    lane = lax.broadcasted_iota(jnp.int32, (heads // 2, 128), 1) % 64
    found = jnp.where(lane == 0, row_peak[0], 0.0)
    found = jnp.where(lane == 1, pltpu.roll(row_total[0], 1, 1), found)
    found = jnp.where(lane == 2, pltpu.roll(row_mean[0], 2, 1), found)
    found = spread(found).astype(BF16)
    for k in range(u_ref.shape[0]):
        u_ref[k, :heads, :] = query_grads
        u_ref[k, heads:, :] = found


def second_kernel(
    heads, group, where_ref, place_ref, x_ref, u_ref, k_ref, v_ref, w_ref, own_ref, other_ref
):
    rows = x_ref.shape[0]
    slots = k_ref.shape[0]
    half = slots // 2
    core, span, row_total = (where_ref[1], where_ref[2], where_ref[3])
    within = lax.broadcasted_iota(jnp.int32, (half, 1), 0).astype(F32)
    position = jnp.concatenate(
        [
            jnp.where(within < place_ref[2], place_ref[0] + within, DEAD),
            jnp.where(within < place_ref[3], place_ref[1] + within, DEAD),
        ],
        axis=0,
    )
    wide = group * heads
    index = lax.broadcasted_iota(jnp.int32, (1, wide), 1) // heads
    stats = gathered_parts(u_ref[:, heads:, :])
    keys = k_ref[...]
    values = v_ref[...]
    value_grads = jnp.zeros((slots, HEAD_WIDTH), F32)
    key_grads = jnp.zeros((slots, HEAD_WIDTH), F32)
    for first in range(0, rows, group):
        part = pl.ds(first, group)
        q = x_ref[part, :heads, :].reshape(wide, HEAD_WIDTH)
        g = x_ref[part, heads : 2 * heads, :].reshape(wide, HEAD_WIDTH)
        held = stats[first : first + group]
        held = jnp.concatenate([held, pltpu.roll(held, 64, 2)], axis=1).reshape(wide, 128)
        turned = jnp.transpose(held)
        asked = (span * row_total + 2 * (first + index) + core).astype(F32)
        scores = rows_dot(keys, q) * SCALE
        raised = jnp.exp(jnp.where(position <= asked, scores - turned[0:1], LOWEST_SCORE))
        weights = raised * (1.0 / turned[1:2])
        score_grads = weights * (rows_dot(values, g) - turned[2:3])
        value_grads += plain_dot(weights.astype(BF16), g)
        key_grads += plain_dot(score_grads.astype(BF16), q)
    key_grads *= SCALE
    low = jnp.concatenate([u_ref[:, h, :] for h in range(heads)], axis=1)
    features = w_ref.shape[0] // 2
    both = rows_dot(low, w_ref[...])
    for ref, first in ((own_ref, 0), (other_ref, 1)):
        part = slice(first * half, (first + 1) * half)
        ref[:half, :HEAD_WIDTH] = key_grads[part]
        ref[:half, HEAD_WIDTH:] = value_grads[part]
        ref[half:, :] = jnp.zeros((rows, 2 * HEAD_WIDTH), F32)
        ref[half:, :features] = both[:, first * features : (first + 1) * features]


def finish_kernel(groups, features, where_ref, own_ref, other_ref, k_ref, v_ref, span_ref, *out_refs):
    half = k_ref.shape[0]
    per = span_ref.shape[0] // 2
    sums = (own_ref[:half, :] + other_ref[:half, :]).astype(BF16)
    k_ref[...] = sums[:, :HEAD_WIDTH]
    v_ref[...] = sums[:, HEAD_WIDTH:]
    is_first = where_ref[1] == 0
    lane = lax.broadcasted_iota(jnp.int32, (2 * per, 128), 1)

    def block_rows(target):
        start = half + per * target
        if per % 8 == 0:
            start = pl.multiple_of(start, 8)
        part = pl.ds(start, per)
        mine, theirs = own_ref[part, :128], other_ref[part, :128]
        even = jnp.where(is_first, mine, theirs)
        odd = jnp.where(is_first, theirs, mine)
        return jnp.where(lane < features, jnp.concatenate([even, odd], axis=0), 0.0)

    mine = where_ref[4]
    span_ref[...] = block_rows(mine)
    for k, ref in enumerate(out_refs, 1):
        high, middle, low = three_parts(block_rows(lax.rem(mine + k, groups)))
        wide = high + pltpu.roll(middle, features, 1) + pltpu.roll(low, 2 * features, 1)
        ref[:half, :] = sums
        ref[half:, :] = jnp.concatenate([wide, jnp.zeros_like(wide)], axis=1).astype(BF16)


def input_kernel(others, sharers, first, more, where_ref, *refs):
    is_first = where_ref[1] == 0
    if first:
        own_ref, own_k_ref, own_v_ref = refs[:3]
    else:
        total_ref, span_ref, *spans = refs[: 2 + more]
    refs = refs[3:] if first else refs[2 + more :]
    arrived, refs = refs[: len(others)], refs[len(others) :]
    here, there, refs = refs[:sharers], refs[sharers : 2 * sharers], refs[2 * sharers :]
    out_ref = refs[0]
    half = out_ref.shape[0]
    left = [own_ref[:half, :]] if first else []
    for ref in arrived:
        keys, values = ref[:half, :HEAD_WIDTH], ref[:half, HEAD_WIDTH:]
        left += [jnp.where(is_first, keys, values), jnp.where(is_first, values, keys)]
    left = jnp.concatenate(left, axis=1)
    share = out_ref.shape[1] // sharers
    for k, (near_ref, far_ref) in enumerate(zip(here, there)):
        start = lax.rem(where_ref[5] - k + sharers, sharers) * share
        part = pl.ds(pl.multiple_of(start, share), share)
        right = [own_k_ref[part, :], own_v_ref[part, :]] if first else []
        for other in others:
            lines = slice((other - 1) * share, other * share)
            right += [near_ref[lines, :], far_ref[lines, :]]
        term = rows_dot(left, jnp.concatenate(right, axis=1))
        out_ref[:, part] = term if first else (total_ref[:, part] + term).astype(BF16)
    if first:
        return
    block_ref, turn_ref = refs[1:3]
    rows, features = block_ref.shape
    span = span_ref[...]
    for ref in (*spans, *arrived):
        wide = ref[half:, :128].astype(F32)
        span += wide + pltpu.roll(wide, 128 - features, 1) + pltpu.roll(wide, 128 - 2 * features, 1)
    turn_ref[pl.ds(0, rows // 2, stride=2), :] = span[: rows // 2]
    turn_ref[pl.ds(1, rows // 2, stride=2), :] = span[rows // 2 :]
    block_ref[...] = turn_ref[:, :features].astype(BF16)


def exchanged(value, axes):
    return lax.all_to_all(value, axes, split_axis=0, concat_axis=0, tiled=True)


def shifted(value, axis, by):
    count = lax.axis_size(axis)
    return lax.ppermute(value, axis, [(k, (k + by) % count) for k in range(count)])


def local(
    queries,
    grad_output,
    key_cache,
    saved_value_rows,
    lengths,
    span_index,
    w_query,
    key_projection_weight,
    value_projection_weight,
):
    heads = queries.shape[1] // HEAD_WIDTH
    rows = lax.axis_size(FAR)
    block = key_cache.shape[0]
    groups = lax.axis_size("head")
    core = lax.axis_index(CORE)
    far = lax.axis_index(FAR)
    mine = lax.axis_index("head")
    lines = 2 * heads + 8
    group = min(16, rows)

    other_length = shifted(lengths, CORE, 1)
    row = pl.pallas_call(
        functools.partial(pack_kernel, heads),
        out_shape=jax.ShapeDtypeStruct((rows, lines, HEAD_WIDTH), BF16),
        in_specs=[SMEM, SMEM, VMEM, VMEM],
        out_specs=VMEM,
        name="row_pack",
    )(lengths, other_length, queries, grad_output)
    x = exchanged(row, FAR)

    cache = jnp.concatenate([key_cache, saved_value_rows], axis=1)
    other_cache = shifted(cache, CORE, 1)
    keys = jnp.concatenate([key_cache, other_cache[:, :HEAD_WIDTH]], axis=0)
    values = jnp.concatenate([saved_value_rows, other_cache[:, HEAD_WIDTH:]], axis=0)

    features = key_projection_weight.shape[0] // groups
    sharers = lax.axis_size("seq_0")
    share = features // sharers
    first_is_key = core == 0
    half_weights = jnp.where(first_is_key, key_projection_weight, value_projection_weight)
    arriving = []
    for k in range(1, groups):
        start = lax.rem(mine + k, groups) * features + lax.axis_index("seq_0") * share
        piece = lax.dynamic_slice_in_dim(half_weights, start, share, 0)
        arriving.append(shifted(piece, "head", k))
    near = [jnp.concatenate(arriving, axis=0)]
    for k in range(1, sharers):
        near.append(shifted(near[0], "seq_0", k))
    there = []
    for piece in near:
        there.append(shifted(piece, CORE, 1))
    own_weights = [
        lax.dynamic_slice_in_dim(w, mine * features, features, 0)
        for w in (key_projection_weight, value_projection_weight)
    ]
    other_query = shifted(w_query, CORE, 1)
    both_query = jnp.concatenate([w_query, other_query], axis=0)

    where = jnp.full((8,), 2 * rows, jnp.int32)
    for k, number in ((0, far), (1, core), (2, span_index[0]), (4, mine), (5, lax.axis_index("seq_0"))):
        where = jnp.where(jnp.arange(8) == k, number, where)
    y, place = pl.pallas_call(
        functools.partial(first_kernel, heads, group),
        out_shape=(
            jax.ShapeDtypeStruct((rows, lines, HEAD_WIDTH), BF16),
            jax.ShapeDtypeStruct((4,), F32),
        ),
        in_specs=[SMEM, VMEM, VMEM, VMEM],
        out_specs=(VMEM, SMEM),
        name="row_partials",
        compiler_params=PARAMS,
    )(where, x, keys, values)
    arrived = exchanged(y, FAR)
    merged = pl.pallas_call(
        functools.partial(merge_kernel, heads),
        out_shape=jax.ShapeDtypeStruct((rows, heads + 8, HEAD_WIDTH), BF16),
        in_specs=[VMEM],
        out_specs=VMEM,
        name="row_merge",
        compiler_params=PARAMS,
    )(arrived)
    u = exchanged(merged, FAR)
    width = w_query.shape[0]
    own_part, other_part = pl.pallas_call(
        functools.partial(second_kernel, heads, group),
        out_shape=(jax.ShapeDtypeStruct((block + rows, 2 * HEAD_WIDTH), F32),) * 2,
        in_specs=[SMEM, SMEM, VMEM, VMEM, VMEM, VMEM, VMEM],
        out_specs=(VMEM, VMEM),
        name="slot_gradients",
        compiler_params=PARAMS,
    )(where, place, x, u, keys, values, both_query)
    other_sums = shifted(other_part, CORE, 1)
    per = rows // groups
    saved_key_gradient, saved_value_gradient, own_span, *leaving = pl.pallas_call(
        functools.partial(finish_kernel, groups, width),
        out_shape=(
            jax.ShapeDtypeStruct((block, HEAD_WIDTH), BF16),
            jax.ShapeDtypeStruct((block, HEAD_WIDTH), BF16),
            jax.ShapeDtypeStruct((2 * per, 128), F32),
        )
        + (jax.ShapeDtypeStruct((block + 2 * per, 2 * HEAD_WIDTH), BF16),) * (groups - 1),
        in_specs=[SMEM, VMEM, VMEM],
        out_specs=(VMEM,) * (2 + groups),
        name="slot_sums",
        compiler_params=PARAMS,
    )(where, own_part, other_sums)

    pieces = {}
    for k, piece in enumerate(leaving, 1):
        pieces[k] = shifted(piece, "head", k)
    early = [k for k in pieces if k != 2]
    total = pl.pallas_call(
        functools.partial(input_kernel, early, sharers, True, 0),
        out_shape=jax.ShapeDtypeStruct((block, features), F32),
        in_specs=[SMEM] + [VMEM] * (3 + len(early) + 2 * sharers),
        out_specs=VMEM,
        name="input_first",
        compiler_params=PARAMS,
    )(where, leaving[0], *own_weights, *[pieces[k] for k in early], *near, *there)
    cached_input_gradient, grad_span_input = pl.pallas_call(
        functools.partial(input_kernel, [2], sharers, False, len(early)),
        out_shape=(
            jax.ShapeDtypeStruct((block, features), BF16),
            jax.ShapeDtypeStruct((2 * per, width), BF16),
        ),
        in_specs=[SMEM] + [VMEM] * (3 + len(early) + 2 * sharers),
        out_specs=(VMEM, VMEM),
        scratch_shapes=[pltpu.VMEM((2 * per, 128), F32)],
        name="input_gradient",
        compiler_params=PARAMS,
    )(where, total, own_span, *[pieces[k] for k in early], pieces[2], *near, *there)
    return (saved_key_gradient, saved_value_gradient, cached_input_gradient, grad_span_input)


def solution(mesh):
    split = Mesh(
        mesh.devices.reshape(4, 8, 2, 2, mesh.shape["head"]),
        ("seq_0", "seq_1", "seq_2", "seq_3", "head"),
    )
    in_specs = (
        P(SEQ, "head"),
        P(SEQ, "head"),
        P(SEQ, "head"),
        P(SEQ, "head"),
        P(SEQ),
        P(),
        P(SEQ, "head"),
        P(None, "head"),
        P(None, "head"),
    )
    out_specs = (P(SEQ, "head"), P(SEQ, "head"), P(SEQ, "head"), P("head", SEQ))
    return jax.shard_map(local, mesh=split, in_specs=in_specs, out_specs=out_specs, check_vma=False)
```

```python
import functools

import jax
import jax.numpy as jnp
from jax import lax
from jax.experimental import pallas as pl
from jax.experimental.pallas import tpu as pltpu
from jax.sharding import Mesh
from jax.sharding import PartitionSpec as P

HEAD_WIDTH = 128
SEQ = ("seq_0", "seq_1", "seq_2", "seq_3")
FAR = ("seq_0", "seq_1")
TEAM = ("seq_2", "seq_3")
MEMBERS = 4
LOWEST_SCORE = -1e30
LOWEST_PEAK = -1e29
DEAD = 1e9
SCALE = HEAD_WIDTH ** (-0.5)
F32 = jnp.float32
BF16 = jnp.bfloat16
VMEM = pl.BlockSpec(memory_space=pltpu.VMEM)
PARAMS = pltpu.CompilerParams(vmem_limit_bytes=32 * 1024 * 1024)
SMEM = pl.BlockSpec(memory_space=pltpu.SMEM)


def rows_dot(a, b):
    return lax.dot_general(a, b, (((1,), (1,)), ((), ())), preferred_element_type=F32)


def plain_dot(a, b):
    return lax.dot_general(a, b, (((1,), (0,)), ((), ())), preferred_element_type=F32)


def three_parts(value):
    high = value.astype(BF16).astype(F32)
    rest = value - high
    middle = rest.astype(BF16).astype(F32)
    low = (rest - middle).astype(BF16).astype(F32)
    return high, middle, low


def spread(held):
    axis = held.ndim - 1
    high, middle, low = three_parts(held)
    return high + pltpu.roll(middle, 16, axis) + pltpu.roll(low, 32, axis)


def gathered_parts(block):
    wide = block.astype(F32)
    axis = wide.ndim - 1
    return wide + pltpu.roll(wide, 112, axis) + pltpu.roll(wide, 96, axis)


def pack_kernel(heads, *refs):
    length_refs, (q_ref, g_ref, row_ref) = refs[:MEMBERS], refs[MEMBERS:]
    lane = lax.broadcasted_iota(jnp.int32, (8, 128), 1)
    numbers = jnp.zeros((8, 128), jnp.int32)
    for e, ref in enumerate(length_refs):
        numbers += jnp.where(lane == 2 * e, ref[0] // 16, 0)
        numbers += jnp.where(lane == 2 * e + 1, ref[0] % 16, 0)
    lines = []
    for ref in (q_ref, g_ref):
        wide = ref[...].astype(F32)
        lines += [wide[:, h * HEAD_WIDTH : (h + 1) * HEAD_WIDTH] for h in range(heads)]
    row = jnp.concatenate([*lines, numbers.astype(F32)], axis=0).astype(BF16)
    for k in range(row_ref.shape[0]):
        row_ref[k] = row


def first_kernel(heads, group, where_ref, x_ref, *refs):
    cache_refs, (y_ref, place_ref) = refs[:MEMBERS], refs[MEMBERS:]
    rows = x_ref.shape[0]
    block = cache_refs[0].shape[0]
    far, team, span, row_total = (where_ref[0], where_ref[1], where_ref[2], where_ref[3])
    lens = x_ref[:, 2 * heads :, :].astype(F32)
    lane = lax.broadcasted_iota(jnp.int32, lens.shape, 2)
    row = lax.broadcasted_iota(jnp.int32, lens.shape, 0)
    first_line = lax.broadcasted_iota(jnp.int32, lens.shape, 1) == 0
    used = first_line & (lane < 2 * MEMBERS)
    lens = lens * jnp.where(used, jnp.where(lane % 2 == 0, 16.0, 1.0), 0.0)
    base = jnp.sum(jnp.where(row < far, lens, 0.0))
    here = jnp.where(row == far, lens, 0.0)
    held = [jnp.sum(jnp.where(lane // 2 == e, here, 0.0)) for e in range(MEMBERS)]
    within = lax.broadcasted_iota(jnp.int32, (1, block), 1).astype(F32)
    position = []
    for e in range(MEMBERS):
        offset = base
        for other in range(MEMBERS):
            offset += jnp.where((team ^ other) < (team ^ e), held[other], 0.0)
        place_ref[e] = offset
        place_ref[MEMBERS + e] = held[e]
        position.append(jnp.where(within < held[e], offset + within, DEAD))
    position = jnp.concatenate(position, axis=1)
    tall = group * heads
    index = lax.broadcasted_iota(jnp.int32, (tall, 1), 0) // heads
    lane = lax.broadcasted_iota(jnp.int32, (tall, 128), 1)
    keys = jnp.concatenate([ref[:, :HEAD_WIDTH] for ref in cache_refs], axis=0)
    values = jnp.concatenate([ref[:, HEAD_WIDTH:] for ref in cache_refs], axis=0)
    for first in range(0, rows, group):
        part = pl.ds(first, group)
        q = x_ref[part, :heads, :].reshape(tall, HEAD_WIDTH)
        g = x_ref[part, heads : 2 * heads, :].reshape(tall, HEAD_WIDTH)
        asked = (span * row_total + MEMBERS * (first + index) + team).astype(F32)
        scores = jnp.where(position <= asked, rows_dot(q, keys) * SCALE, LOWEST_SCORE)
        peak = jnp.maximum(jnp.max(scores, axis=1, keepdims=True), LOWEST_PEAK)
        raised = jnp.exp(scores - peak)
        grads = rows_dot(g, values)
        total = jnp.sum(raised, axis=1, keepdims=True)
        mean = jnp.sum(raised * grads, axis=1, keepdims=True) / jnp.maximum(total, 0.5)
        moved = (raised * (grads - mean)).astype(BF16)
        both = plain_dot(jnp.concatenate([moved, raised.astype(BF16)], axis=0), keys)
        y_ref[part, :heads, :] = both[:tall].astype(BF16).reshape(group, heads, HEAD_WIDTH)
        y_ref[part, heads : 2 * heads, :] = both[tall:].astype(BF16).reshape(group, heads, HEAD_WIDTH)
        held = jnp.where(lane == 0, peak, jnp.where(lane == 1, total, jnp.where(lane == 2, mean, 0.0)))
        held = spread(held).reshape(group, 2, heads // 2, 128)
        held = held[:, 0] + pltpu.roll(held[:, 1], 64, 2)
        y_ref[part, 2 * heads :, :] = held.astype(BF16)


def merge_kernel(heads, z_ref, u_ref):
    stats = gathered_parts(z_ref[:, 2 * heads :, :])
    total = pltpu.roll(stats, 127, 2)
    mean = pltpu.roll(stats, 126, 2)
    row_peak = jnp.max(stats, axis=0, keepdims=True)
    share = jnp.exp(stats - row_peak)
    part = share * total
    row_total = jnp.sum(part, axis=0, keepdims=True)
    row_mean = jnp.sum(part * mean, axis=0, keepdims=True) / row_total
    moved_factor = share * (SCALE / row_total)
    plain_factor = moved_factor * (mean - row_mean)

    def of_heads(factor):
        return jnp.concatenate([factor[:, :, 0:1], factor[:, :, 64:65]], axis=1)

    term = z_ref[:, :heads, :].astype(F32) * of_heads(moved_factor)
    term += z_ref[:, heads : 2 * heads, :].astype(F32) * of_heads(plain_factor)
    query_grads = jnp.sum(term, axis=0).astype(BF16)
    lane = lax.broadcasted_iota(jnp.int32, (heads // 2, 128), 1) % 64
    found = jnp.where(lane == 0, row_peak[0], 0.0)
    found = jnp.where(lane == 1, pltpu.roll(row_total[0], 1, 1), found)
    found = jnp.where(lane == 2, pltpu.roll(row_mean[0], 2, 1), found)
    found = spread(found).astype(BF16)
    for k in range(u_ref.shape[0]):
        u_ref[k, :heads, :] = query_grads
        u_ref[k, heads:, :] = found


def second_kernel(heads, group, where_ref, place_ref, x_ref, u_ref, *refs):
    cache_refs, w_refs = refs[:MEMBERS], refs[MEMBERS : 2 * MEMBERS]
    keep_ref, send_ref = refs[2 * MEMBERS :]
    rows = x_ref.shape[0]
    block = cache_refs[0].shape[0]
    slots = MEMBERS * block
    team, span, row_total = (where_ref[1], where_ref[2], where_ref[3])
    within = lax.broadcasted_iota(jnp.int32, (block, 1), 0).astype(F32)
    position = jnp.concatenate(
        [
            jnp.where(within < place_ref[MEMBERS + e], place_ref[e] + within, DEAD)
            for e in range(MEMBERS)
        ],
        axis=0,
    )
    wide = group * heads
    index = lax.broadcasted_iota(jnp.int32, (1, wide), 1) // heads
    stats = gathered_parts(u_ref[:, heads:, :])
    keys = jnp.concatenate([ref[:, :HEAD_WIDTH] for ref in cache_refs], axis=0)
    values = jnp.concatenate([ref[:, HEAD_WIDTH:] for ref in cache_refs], axis=0)
    value_grads = jnp.zeros((slots, HEAD_WIDTH), F32)
    key_grads = jnp.zeros((slots, HEAD_WIDTH), F32)
    for first in range(0, rows, group):
        part = pl.ds(first, group)
        q = x_ref[part, :heads, :].reshape(wide, HEAD_WIDTH)
        g = x_ref[part, heads : 2 * heads, :].reshape(wide, HEAD_WIDTH)
        held = stats[first : first + group]
        held = jnp.concatenate([held, pltpu.roll(held, 64, 2)], axis=1).reshape(wide, 128)
        turned = jnp.transpose(held)
        asked = (span * row_total + MEMBERS * (first + index) + team).astype(F32)
        scores = rows_dot(keys, q) * SCALE
        raised = jnp.exp(jnp.where(position <= asked, scores - turned[0:1], LOWEST_SCORE))
        weights = raised * (1.0 / turned[1:2])
        score_grads = weights * (rows_dot(values, g) - turned[2:3])
        value_grads += plain_dot(weights.astype(BF16), g)
        key_grads += plain_dot(score_grads.astype(BF16), q)
    key_grads *= SCALE
    low = jnp.concatenate([u_ref[:, h, :] for h in range(heads)], axis=1)
    features = w_refs[0].shape[0]
    both = rows_dot(low, jnp.concatenate([ref[...] for ref in w_refs], axis=0))
    for e in range(MEMBERS):
        ref, at = (keep_ref, send_ref)[e % 2], e // 2
        part = slice(e * block, (e + 1) * block)
        ref[at, :block, :HEAD_WIDTH] = key_grads[part]
        ref[at, :block, HEAD_WIDTH:] = value_grads[part]
        ref[at, block:, :] = jnp.zeros((rows, 2 * HEAD_WIDTH), F32)
        ref[at, block:, :features] = both[:, e * features : (e + 1) * features]


def joined_parts(value, features):
    lane = lax.broadcasted_iota(jnp.int32, value.shape, 1)
    high, middle, low = three_parts(jnp.where(lane < features, value, 0.0))
    wide = high + pltpu.roll(middle, features, 1) + pltpu.roll(low, 2 * features, 1)
    return jnp.concatenate([wide, jnp.zeros_like(wide)], axis=1).astype(BF16)


def split_parts(block, features):
    wide = block[:, :128].astype(F32)
    return wide + pltpu.roll(wide, 128 - features, 1) + pltpu.roll(wide, 128 - 2 * features, 1)


def core_kernel(block, features, keep_ref, other_ref, stay_ref, leave_ref):
    rows = keep_ref.shape[1] - block
    stay_ref[:block, :] = keep_ref[0, :block, :] + other_ref[0, :block, :]
    stay_ref[block : block + rows, :] = keep_ref[0, block:, :]
    stay_ref[block + rows :, :] = other_ref[0, block:, :]
    leave_ref[:block, :] = (keep_ref[1, :block, :] + other_ref[1, :block, :]).astype(BF16)
    leave_ref[block : block + rows, :] = joined_parts(keep_ref[1, block:, :128], features)
    leave_ref[block + rows :, :] = joined_parts(other_ref[1, block:, :128], features)


def finish_kernel(
    groups, features, where_ref, stay_ref, other_ref, k_ref, v_ref, span_ref, *out_refs
):
    out_refs, lines_ref = out_refs[:-1], out_refs[-1]
    block = k_ref.shape[0]
    rows = (stay_ref.shape[0] - block) // 2
    per = rows // groups
    sums = (stay_ref[:block, :] + other_ref[:block, :].astype(F32)).astype(BF16)
    k_ref[...] = sums[:, :HEAD_WIDTH]
    v_ref[...] = sums[:, HEAD_WIDTH:]
    team, mine = where_ref[1], where_ref[4]
    lane = lax.broadcasted_iota(jnp.int32, (rows, 128), 1)
    apart = [stay_ref[block : block + rows, :128], stay_ref[block + rows :, :128]]
    apart += [
        split_parts(other_ref[block : block + rows, :], features),
        split_parts(other_ref[block + rows :, :], features),
    ]
    for member in range(MEMBERS):
        value = apart[0]
        for e in range(1, MEMBERS):
            value = jnp.where((team ^ e) == member, apart[e], value)
        lines_ref[member, :, :] = jnp.where(lane < features, value, 0.0)

    def block_rows(target):
        start = per * target
        if per % 8 == 0:
            start = pl.multiple_of(start, 8)
        part = pl.ds(start, per)
        return jnp.concatenate([lines_ref[m, part, :] for m in range(MEMBERS)], axis=0)

    span_ref[...] = block_rows(mine)
    for k, ref in enumerate(out_refs, 1):
        ref[:block, :] = sums
        ref[block:, :] = joined_parts(block_rows(lax.rem(mine + k, groups)), features)


def input_kernel(others, groups, first, where_ref, *refs):
    is_first = where_ref[5] == 0
    count = len(others)
    if first:
        (own_ref, own_k_ref, own_v_ref), refs = refs[:3], refs[3:]
    else:
        total_ref, span_ref, *spans = refs[: groups]
        refs = refs[groups:]
    arrived, here, there = (refs[:count], refs[count : 2 * count], refs[2 * count : 3 * count])
    refs = refs[3 * count :]
    out_ref = refs[0]
    half = out_ref.shape[0]
    left = [own_ref[:half, :]] if first else []
    for ref in arrived:
        keys, values = ref[:half, :HEAD_WIDTH], ref[:half, HEAD_WIDTH:]
        left += [jnp.where(is_first, keys, values), jnp.where(is_first, values, keys)]
    left = jnp.concatenate(left, axis=1)
    step = min(256, out_ref.shape[1])
    for start in range(0, out_ref.shape[1], step):
        part = pl.ds(start, step)
        right = [own_k_ref[part, :], own_v_ref[part, :]] if first else []
        for near_ref, far_ref in zip(here, there):
            right += [near_ref[part, :], far_ref[part, :]]
        term = rows_dot(left, jnp.concatenate(right, axis=1))
        out_ref[:, part] = term if first else (total_ref[:, part] + term).astype(BF16)
    if first:
        return
    block_ref, turn_ref = refs[1:3]
    rows, features = block_ref.shape
    span = span_ref[...]
    for ref in (*spans, *arrived):
        span += split_parts(ref[half:, :], features)
    per = rows // MEMBERS
    for member in range(MEMBERS):
        turn_ref[pl.ds(member, per, stride=MEMBERS), :] = span[member * per : (member + 1) * per]
    block_ref[...] = turn_ref[:, :features].astype(BF16)


def exchanged(value, axes):
    return lax.all_to_all(value, axes, split_axis=0, concat_axis=0, tiled=True)


def shifted(value, axis, by):
    count = lax.axis_size(axis)
    return lax.ppermute(value, axis, [(k, (k + by) % count) for k in range(count)])


def partner(value, distance):
    return lax.ppermute(value, TEAM, [(k, k ^ distance) for k in range(MEMBERS)])


def local(
    queries,
    grad_output,
    key_cache,
    saved_value_rows,
    lengths,
    span_index,
    w_query,
    key_projection_weight,
    value_projection_weight,
):
    heads = queries.shape[1] // HEAD_WIDTH
    rows = lax.axis_size(FAR)
    block = key_cache.shape[0]
    groups = lax.axis_size("head")
    team = lax.axis_index(TEAM)
    core = lax.axis_index("seq_3")
    far = lax.axis_index(FAR)
    mine = lax.axis_index("head")
    lines = 2 * heads + 8
    group = min(8, rows)

    lens = [lengths]
    for e in range(1, MEMBERS):
        lens.append(partner(lengths, e))
    row = pl.pallas_call(
        functools.partial(pack_kernel, heads),
        out_shape=jax.ShapeDtypeStruct((rows, lines, HEAD_WIDTH), BF16),
        in_specs=[SMEM] * MEMBERS + [VMEM, VMEM],
        out_specs=VMEM,
        name="row_pack",
    )(*lens, queries, grad_output)
    x = exchanged(row, FAR)

    cache = jnp.concatenate([key_cache, saved_value_rows], axis=1)
    cache_2 = partner(cache, 2)
    cache_1 = partner(cache, 1)
    cache_3 = partner(cache_2, 1)
    caches = (cache, cache_1, cache_2, cache_3)

    features = key_projection_weight.shape[0] // groups
    half_weights = jnp.where(core == 0, key_projection_weight, value_projection_weight)
    near, there = {}, {}
    for k in range(1, groups):
        start = lax.rem(mine + k, groups) * features
        piece = lax.dynamic_slice_in_dim(half_weights, start, features, 0)
        near[k] = shifted(piece, "head", k)
        there[k] = partner(near[k], 1)
    own_weights = [
        lax.dynamic_slice_in_dim(w, mine * features, features, 0)
        for w in (key_projection_weight, value_projection_weight)
    ]
    query_2 = partner(w_query, 2)
    query_1 = partner(w_query, 1)
    query_3 = partner(query_2, 1)
    query_weights = (w_query, query_1, query_2, query_3)

    where = jnp.full((8,), MEMBERS * rows, jnp.int32)
    for k, number in ((0, far), (1, team), (2, span_index[0]), (4, mine), (5, core)):
        where = jnp.where(jnp.arange(8) == k, number, where)
    y, place = pl.pallas_call(
        functools.partial(first_kernel, heads, group),
        out_shape=(
            jax.ShapeDtypeStruct((rows, lines, HEAD_WIDTH), BF16),
            jax.ShapeDtypeStruct((2 * MEMBERS,), F32),
        ),
        in_specs=[SMEM] + [VMEM] * (1 + MEMBERS),
        out_specs=(VMEM, SMEM),
        name="row_partials",
        compiler_params=PARAMS,
    )(where, x, *caches)
    arrived = exchanged(y, FAR)
    merged = pl.pallas_call(
        functools.partial(merge_kernel, heads),
        out_shape=jax.ShapeDtypeStruct((rows, heads + 8, HEAD_WIDTH), BF16),
        in_specs=[VMEM],
        out_specs=VMEM,
        name="row_merge",
        compiler_params=PARAMS,
    )(arrived)
    u = exchanged(merged, FAR)
    width = w_query.shape[0]
    slot_call = pl.pallas_call(
        functools.partial(second_kernel, heads, min(16, rows)),
        out_shape=(jax.ShapeDtypeStruct((2, block + rows, 2 * HEAD_WIDTH), F32),) * 2,
        in_specs=[SMEM, SMEM] + [VMEM] * (2 + 2 * MEMBERS),
        out_specs=(VMEM, VMEM),
        name="slot_gradients",
        compiler_params=PARAMS,
    )
    kept, crossing = slot_call(where, place, x, u, *caches, *query_weights)
    other_core = partner(crossing, 1)
    stay, leave = pl.pallas_call(
        functools.partial(core_kernel, block, width),
        out_shape=(
            jax.ShapeDtypeStruct((block + 2 * rows, 2 * HEAD_WIDTH), F32),
            jax.ShapeDtypeStruct((block + 2 * rows, 2 * HEAD_WIDTH), BF16),
        ),
        in_specs=[VMEM, VMEM],
        out_specs=(VMEM, VMEM),
        name="core_sums",
        compiler_params=PARAMS,
    )(kept, other_core)
    other_chip = partner(leave, 2)
    per = rows // groups
    saved_key_gradient, saved_value_gradient, own_span, *leaving = pl.pallas_call(
        functools.partial(finish_kernel, groups, width),
        out_shape=(
            jax.ShapeDtypeStruct((block, HEAD_WIDTH), BF16),
            jax.ShapeDtypeStruct((block, HEAD_WIDTH), BF16),
            jax.ShapeDtypeStruct((MEMBERS * per, 128), F32),
        )
        + (jax.ShapeDtypeStruct((block + MEMBERS * per, 2 * HEAD_WIDTH), BF16),) * (groups - 1),
        in_specs=[SMEM, VMEM, VMEM],
        out_specs=(VMEM,) * (2 + groups),
        scratch_shapes=[pltpu.VMEM((MEMBERS, rows, 128), F32)],
        name="slot_sums",
        compiler_params=PARAMS,
    )(where, stay, other_chip)

    pieces = {}
    for k, piece in enumerate(leaving, 1):
        pieces[k] = shifted(piece, "head", k)
    early = [k for k in pieces if k != 2]
    of = lambda held, wanted: [held[k] for k in wanted]
    total = pl.pallas_call(
        functools.partial(input_kernel, early, groups, True),
        out_shape=jax.ShapeDtypeStruct((block, features), F32),
        in_specs=[SMEM] + [VMEM] * (3 + 3 * len(early)),
        out_specs=VMEM,
        name="input_first",
        compiler_params=PARAMS,
    )(where, leaving[0], *own_weights, *of(pieces, early), *of(near, early), *of(there, early))
    cached_input_gradient, grad_span_input = pl.pallas_call(
        functools.partial(input_kernel, [2], groups, False),
        out_shape=(
            jax.ShapeDtypeStruct((block, features), BF16),
            jax.ShapeDtypeStruct((MEMBERS * per, width), BF16),
        ),
        in_specs=[SMEM] + [VMEM] * (groups + 3),
        out_specs=(VMEM, VMEM),
        scratch_shapes=[pltpu.VMEM((MEMBERS * per, 128), F32)],
        name="input_gradient",
        compiler_params=PARAMS,
    )(where, total, own_span, *of(pieces, early), pieces[2], near[2], there[2])
    return (saved_key_gradient, saved_value_gradient, cached_input_gradient, grad_span_input)


def solution(mesh):
    split = Mesh(
        mesh.devices.reshape(4, 8, 2, 2, mesh.shape["head"]),
        ("seq_0", "seq_1", "seq_2", "seq_3", "head"),
    )
    in_specs = (
        P(SEQ, "head"),
        P(SEQ, "head"),
        P(SEQ, "head"),
        P(SEQ, "head"),
        P(SEQ),
        P(),
        P(SEQ, "head"),
        P(None, "head"),
        P(None, "head"),
    )
    out_specs = (P(SEQ, "head"), P(SEQ, "head"), P(SEQ, "head"), P("head", SEQ))
    return jax.shard_map(local, mesh=split, in_specs=in_specs, out_specs=out_specs, check_vma=False)
```

```python
import functools

import jax
import jax.numpy as jnp
from jax import lax
from jax.experimental import pallas as pl
from jax.experimental.pallas import tpu as pltpu
from jax.sharding import Mesh
from jax.sharding import PartitionSpec as P

HEAD_WIDTH = 128
SEQ = ("seq_0", "seq_1", "seq_2", "seq_3")
FAR = ("seq_0", "seq_1", "seq_2")
CORE = "seq_3"
LOWEST_SCORE = -1e30
LOWEST_PEAK = -1e29
DEAD = 1e9
SCALE = HEAD_WIDTH ** (-0.5)
F32 = jnp.float32
BF16 = jnp.bfloat16
VMEM = pl.BlockSpec(memory_space=pltpu.VMEM)
PARAMS = pltpu.CompilerParams(vmem_limit_bytes=32 * 1024 * 1024)
SMEM = pl.BlockSpec(memory_space=pltpu.SMEM)


def rows_dot(a, b):
    return lax.dot_general(a, b, (((1,), (1,)), ((), ())), preferred_element_type=F32)


def plain_dot(a, b):
    return lax.dot_general(a, b, (((1,), (0,)), ((), ())), preferred_element_type=F32)


def three_parts(value):
    high = value.astype(BF16).astype(F32)
    rest = value - high
    middle = rest.astype(BF16).astype(F32)
    low = (rest - middle).astype(BF16).astype(F32)
    return high, middle, low


def spread(held):
    axis = held.ndim - 1
    high, middle, low = three_parts(held)
    return high + pltpu.roll(middle, 16, axis) + pltpu.roll(low, 32, axis)


def gathered_parts(block):
    wide = block.astype(F32)
    axis = wide.ndim - 1
    return wide + pltpu.roll(wide, 112, axis) + pltpu.roll(wide, 96, axis)


def pack_kernel(heads, own_ref, other_ref, q_ref, g_ref, row_ref):
    lane = lax.broadcasted_iota(jnp.int32, (8, 128), 1)
    own, other = own_ref[0], other_ref[0]
    numbers = jnp.where(lane == 0, own // 16, 0) + jnp.where(lane == 1, own % 16, 0)
    numbers += jnp.where(lane == 2, other // 16, 0) + jnp.where(lane == 3, other % 16, 0)
    lines = []
    for ref in (q_ref, g_ref):
        wide = ref[...].astype(F32)
        lines += [wide[:, h * HEAD_WIDTH : (h + 1) * HEAD_WIDTH] for h in range(heads)]
    row = jnp.concatenate([*lines, numbers.astype(F32)], axis=0).astype(BF16)
    for k in range(row_ref.shape[0]):
        row_ref[k] = row


def first_kernel(heads, group, where_ref, x_ref, k_ref, v_ref, y_ref, place_ref):
    rows = x_ref.shape[0]
    half = k_ref.shape[0] // 2
    far, core, span, row_total = (where_ref[0], where_ref[1], where_ref[2], where_ref[3])
    lens = x_ref[:, 2 * heads :, :].astype(F32)
    lane = lax.broadcasted_iota(jnp.int32, lens.shape, 2)
    row = lax.broadcasted_iota(jnp.int32, lens.shape, 0)
    first_line = lax.broadcasted_iota(jnp.int32, lens.shape, 1) == 0
    lens = lens * jnp.where(first_line & (lane < 4), jnp.where(lane % 2 == 0, 16.0, 1.0), 0.0)
    base = jnp.sum(jnp.where(row < far, lens, 0.0))
    here = jnp.where(row == far, lens, 0.0)
    own = jnp.sum(jnp.where(lane < 2, here, 0.0))
    other = jnp.sum(jnp.where(lane >= 2, here, 0.0))
    is_second = core.astype(F32)
    own_offset = base + is_second * other
    other_offset = base + (1.0 - is_second) * own
    place_ref[0] = own_offset
    place_ref[1] = other_offset
    place_ref[2] = own
    place_ref[3] = other
    within = lax.broadcasted_iota(jnp.int32, (1, half), 1).astype(F32)
    position = jnp.concatenate(
        [
            jnp.where(within < own, own_offset + within, DEAD),
            jnp.where(within < other, other_offset + within, DEAD),
        ],
        axis=1,
    )
    tall = group * heads
    index = lax.broadcasted_iota(jnp.int32, (tall, 1), 0) // heads
    lane = lax.broadcasted_iota(jnp.int32, (tall, 128), 1)
    keys = k_ref[...]
    values = v_ref[...]
    for first in range(0, rows, group):
        part = pl.ds(first, group)
        q = x_ref[part, :heads, :].reshape(tall, HEAD_WIDTH)
        g = x_ref[part, heads : 2 * heads, :].reshape(tall, HEAD_WIDTH)
        asked = (span * row_total + 2 * (first + index) + core).astype(F32)
        scores = jnp.where(position <= asked, rows_dot(q, keys) * SCALE, LOWEST_SCORE)
        peak = jnp.maximum(jnp.max(scores, axis=1, keepdims=True), LOWEST_PEAK)
        raised = jnp.exp(scores - peak)
        grads = rows_dot(g, values)
        total = jnp.sum(raised, axis=1, keepdims=True)
        mean = jnp.sum(raised * grads, axis=1, keepdims=True) / jnp.maximum(total, 0.5)
        moved = (raised * (grads - mean)).astype(BF16)
        both = plain_dot(jnp.concatenate([moved, raised.astype(BF16)], axis=0), keys)
        y_ref[part, :heads, :] = both[:tall].astype(BF16).reshape(group, heads, HEAD_WIDTH)
        y_ref[part, heads : 2 * heads, :] = both[tall:].astype(BF16).reshape(group, heads, HEAD_WIDTH)
        held = jnp.where(lane == 0, peak, jnp.where(lane == 1, total, jnp.where(lane == 2, mean, 0.0)))
        held = spread(held).reshape(group, 2, heads // 2, 128)
        held = held[:, 0] + pltpu.roll(held[:, 1], 64, 2)
        y_ref[part, 2 * heads :, :] = held.astype(BF16)


def merge_kernel(heads, z_ref, u_ref):
    stats = gathered_parts(z_ref[:, 2 * heads :, :])
    total = pltpu.roll(stats, 127, 2)
    mean = pltpu.roll(stats, 126, 2)
    row_peak = jnp.max(stats, axis=0, keepdims=True)
    share = jnp.exp(stats - row_peak)
    part = share * total
    row_total = jnp.sum(part, axis=0, keepdims=True)
    row_mean = jnp.sum(part * mean, axis=0, keepdims=True) / row_total
    moved_factor = share * (SCALE / row_total)
    plain_factor = moved_factor * (mean - row_mean)

    def of_heads(factor):
        return jnp.concatenate([factor[:, :, 0:1], factor[:, :, 64:65]], axis=1)

    term = z_ref[:, :heads, :].astype(F32) * of_heads(moved_factor)
    term += z_ref[:, heads : 2 * heads, :].astype(F32) * of_heads(plain_factor)
    query_grads = jnp.sum(term, axis=0).astype(BF16)
    lane = lax.broadcasted_iota(jnp.int32, (heads // 2, 128), 1) % 64
    found = jnp.where(lane == 0, row_peak[0], 0.0)
    found = jnp.where(lane == 1, pltpu.roll(row_total[0], 1, 1), found)
    found = jnp.where(lane == 2, pltpu.roll(row_mean[0], 2, 1), found)
    found = spread(found).astype(BF16)
    for k in range(u_ref.shape[0]):
        u_ref[k, :heads, :] = query_grads
        u_ref[k, heads:, :] = found


def second_kernel(
    heads, group, where_ref, place_ref, x_ref, u_ref, k_ref, v_ref, w_ref, own_ref, other_ref
):
    rows = x_ref.shape[0]
    slots = k_ref.shape[0]
    half = slots // 2
    core, span, row_total = (where_ref[1], where_ref[2], where_ref[3])
    within = lax.broadcasted_iota(jnp.int32, (half, 1), 0).astype(F32)
    position = jnp.concatenate(
        [
            jnp.where(within < place_ref[2], place_ref[0] + within, DEAD),
            jnp.where(within < place_ref[3], place_ref[1] + within, DEAD),
        ],
        axis=0,
    )
    wide = group * heads
    index = lax.broadcasted_iota(jnp.int32, (1, wide), 1) // heads
    stats = gathered_parts(u_ref[:, heads:, :])
    keys = k_ref[...]
    values = v_ref[...]
    value_grads = jnp.zeros((slots, HEAD_WIDTH), F32)
    key_grads = jnp.zeros((slots, HEAD_WIDTH), F32)
    for first in range(0, rows, group):
        part = pl.ds(first, group)
        q = x_ref[part, :heads, :].reshape(wide, HEAD_WIDTH)
        g = x_ref[part, heads : 2 * heads, :].reshape(wide, HEAD_WIDTH)
        held = stats[first : first + group]
        held = jnp.concatenate([held, pltpu.roll(held, 64, 2)], axis=1).reshape(wide, 128)
        turned = jnp.transpose(held)
        asked = (span * row_total + 2 * (first + index) + core).astype(F32)
        scores = rows_dot(keys, q) * SCALE
        raised = jnp.exp(jnp.where(position <= asked, scores - turned[0:1], LOWEST_SCORE))
        weights = raised * (1.0 / turned[1:2])
        score_grads = weights * (rows_dot(values, g) - turned[2:3])
        value_grads += plain_dot(weights.astype(BF16), g)
        key_grads += plain_dot(score_grads.astype(BF16), q)
    key_grads *= SCALE
    low = jnp.concatenate([u_ref[:, h, :] for h in range(heads)], axis=1)
    features = w_ref.shape[0] // 2
    both = rows_dot(low, w_ref[...])
    for ref, first in ((own_ref, 0), (other_ref, 1)):
        part = slice(first * half, (first + 1) * half)
        ref[:half, :HEAD_WIDTH] = key_grads[part]
        ref[:half, HEAD_WIDTH:] = value_grads[part]
        ref[half:, :] = jnp.zeros((rows, 2 * HEAD_WIDTH), F32)
        ref[half:, :features] = both[:, first * features : (first + 1) * features]


def folded(value):
    high = value.astype(BF16).astype(F32)
    wide = high + pltpu.roll((value - high).astype(BF16).astype(F32), 32, 1)
    count = value.shape[0] // 4
    a, b, c, d = [wide[k * count : (k + 1) * count] for k in range(4)]
    both = [a + pltpu.roll(b, 64, 1), c + pltpu.roll(d, 64, 1)]
    return jnp.concatenate(both, axis=1).astype(BF16)


def unfolded(block):
    wide = block.astype(F32)
    left, right = wide[:, :128], wide[:, 128:]
    rows = [left, pltpu.roll(left, 64, 1), right, pltpu.roll(right, 64, 1)]
    rows = jnp.concatenate(rows, axis=0)
    return rows + pltpu.roll(rows, 96, 1)


def finish_kernel(groups, features, where_ref, own_ref, other_ref, k_ref, v_ref, send_ref):
    half = k_ref.shape[0]
    per = (own_ref.shape[0] - half) // groups
    sums = (own_ref[:half, :] + other_ref[:half, :]).astype(BF16)
    k_ref[...] = sums[:, :HEAD_WIDTH]
    v_ref[...] = sums[:, HEAD_WIDTH:]
    is_first = where_ref[1] == 0
    lane = lax.broadcasted_iota(jnp.int32, (2 * per, 128), 1)
    for target in range(groups):
        part = slice(half + per * target, half + per * (target + 1))
        mine, theirs = own_ref[part, :128], other_ref[part, :128]
        even = jnp.where(is_first, mine, theirs)
        odd = jnp.where(is_first, theirs, mine)
        lines = jnp.where(lane < features, jnp.concatenate([even, odd], axis=0), 0.0)
        send_ref[target, :half, :] = sums
        send_ref[target, half:, :] = folded(lines)


def input_kernel(groups, sharers, where_ref, arrived_ref, own_k_ref, own_v_ref, *refs):
    here, there, refs = refs[:sharers], refs[sharers : 2 * sharers], refs[2 * sharers :]
    out_ref, block_ref, turn_ref = refs
    half = out_ref.shape[0]
    is_first = where_ref[1] == 0
    mine = where_ref[4]
    left = [arrived_ref[mine, :half, :]]
    span = unfolded(arrived_ref[0, half:, :])
    for k in range(1, groups):
        both = arrived_ref[lax.rem(mine - k + groups, groups), :half, :]
        keys, values = both[:, :HEAD_WIDTH], both[:, HEAD_WIDTH:]
        left += [jnp.where(is_first, keys, values), jnp.where(is_first, values, keys)]
        span += unfolded(arrived_ref[k, half:, :])
    left = jnp.concatenate(left, axis=1)
    share = out_ref.shape[1] // sharers
    for k, (near_ref, far_ref) in enumerate(zip(here, there)):
        start = lax.rem(where_ref[5] - k + sharers, sharers) * share
        part = pl.ds(pl.multiple_of(start, share), share)
        right = [own_k_ref[part, :], own_v_ref[part, :]]
        for other in range(groups - 1):
            lines = slice(other * share, (other + 1) * share)
            right += [near_ref[lines, :], far_ref[lines, :]]
        out_ref[:, part] = rows_dot(left, jnp.concatenate(right, axis=1)).astype(BF16)
    rows, features = block_ref.shape
    turn_ref[pl.ds(0, rows // 2, stride=2), :] = span[: rows // 2]
    turn_ref[pl.ds(1, rows // 2, stride=2), :] = span[rows // 2 :]
    block_ref[...] = turn_ref[:, :features].astype(BF16)


def exchanged(value, axes):
    return lax.all_to_all(value, axes, split_axis=0, concat_axis=0, tiled=True)


def shifted(value, axis, by):
    count = lax.axis_size(axis)
    return lax.ppermute(value, axis, [(k, (k + by) % count) for k in range(count)])


def local(
    queries,
    grad_output,
    key_cache,
    saved_value_rows,
    lengths,
    span_index,
    w_query,
    key_projection_weight,
    value_projection_weight,
):
    heads = queries.shape[1] // HEAD_WIDTH
    rows = lax.axis_size(FAR)
    block = key_cache.shape[0]
    groups = lax.axis_size("head")
    core = lax.axis_index(CORE)
    far = lax.axis_index(FAR)
    mine = lax.axis_index("head")
    lines = 2 * heads + 8
    group = min(16, rows)

    other_length = shifted(lengths, CORE, 1)
    row = pl.pallas_call(
        functools.partial(pack_kernel, heads),
        out_shape=jax.ShapeDtypeStruct((rows, lines, HEAD_WIDTH), BF16),
        in_specs=[SMEM, SMEM, VMEM, VMEM],
        out_specs=VMEM,
        name="row_pack",
    )(lengths, other_length, queries, grad_output)
    x = exchanged(row, FAR)

    cache = jnp.concatenate([key_cache, saved_value_rows], axis=1)
    other_cache = shifted(cache, CORE, 1)
    keys = jnp.concatenate([key_cache, other_cache[:, :HEAD_WIDTH]], axis=0)
    values = jnp.concatenate([saved_value_rows, other_cache[:, HEAD_WIDTH:]], axis=0)

    features = key_projection_weight.shape[0] // groups
    sharers = lax.axis_size("seq_0")
    share = features // sharers
    first_is_key = core == 0
    half_weights = jnp.where(first_is_key, key_projection_weight, value_projection_weight)
    arriving = []
    for k in range(1, groups):
        start = lax.rem(mine + k, groups) * features + lax.axis_index("seq_0") * share
        piece = lax.dynamic_slice_in_dim(half_weights, start, share, 0)
        arriving.append(shifted(piece, "head", k))
    near = [jnp.concatenate(arriving, axis=0)]
    for k in range(1, sharers):
        near.append(shifted(near[0], "seq_0", k))
    there = []
    for piece in near:
        there.append(shifted(piece, CORE, 1))
    own_weights = [
        lax.dynamic_slice_in_dim(w, mine * features, features, 0)
        for w in (key_projection_weight, value_projection_weight)
    ]
    other_query = shifted(w_query, CORE, 1)
    both_query = jnp.concatenate([w_query, other_query], axis=0)

    where = jnp.full((8,), 2 * rows, jnp.int32)
    for k, number in ((0, far), (1, core), (2, span_index[0]), (4, mine), (5, lax.axis_index("seq_0"))):
        where = jnp.where(jnp.arange(8) == k, number, where)
    y, place = pl.pallas_call(
        functools.partial(first_kernel, heads, group),
        out_shape=(
            jax.ShapeDtypeStruct((rows, lines, HEAD_WIDTH), BF16),
            jax.ShapeDtypeStruct((4,), F32),
        ),
        in_specs=[SMEM, VMEM, VMEM, VMEM],
        out_specs=(VMEM, SMEM),
        name="row_partials",
        compiler_params=PARAMS,
    )(where, x, keys, values)
    arrived = exchanged(y, FAR)
    merged = pl.pallas_call(
        functools.partial(merge_kernel, heads),
        out_shape=jax.ShapeDtypeStruct((rows, heads + 8, HEAD_WIDTH), BF16),
        in_specs=[VMEM],
        out_specs=VMEM,
        name="row_merge",
        compiler_params=PARAMS,
    )(arrived)
    u = exchanged(merged, FAR)
    width = w_query.shape[0]
    own_part, other_part = pl.pallas_call(
        functools.partial(second_kernel, heads, group),
        out_shape=(jax.ShapeDtypeStruct((block + rows, 2 * HEAD_WIDTH), F32),) * 2,
        in_specs=[SMEM, SMEM, VMEM, VMEM, VMEM, VMEM, VMEM],
        out_specs=(VMEM, VMEM),
        name="slot_gradients",
        compiler_params=PARAMS,
    )(where, place, x, u, keys, values, both_query)
    other_sums = shifted(other_part, CORE, 1)
    per = rows // groups
    saved_key_gradient, saved_value_gradient, leaving = pl.pallas_call(
        functools.partial(finish_kernel, groups, width),
        out_shape=(
            jax.ShapeDtypeStruct((block, HEAD_WIDTH), BF16),
            jax.ShapeDtypeStruct((block, HEAD_WIDTH), BF16),
            jax.ShapeDtypeStruct((groups, block + per // 2, 2 * HEAD_WIDTH), BF16),
        ),
        in_specs=[SMEM, VMEM, VMEM],
        out_specs=(VMEM, VMEM, VMEM),
        name="slot_sums",
        compiler_params=PARAMS,
    )(where, own_part, other_sums)

    pieces = exchanged(leaving, "head")
    cached_input_gradient, grad_span_input = pl.pallas_call(
        functools.partial(input_kernel, groups, sharers),
        out_shape=(
            jax.ShapeDtypeStruct((block, features), BF16),
            jax.ShapeDtypeStruct((2 * per, width), BF16),
        ),
        in_specs=[SMEM] + [VMEM] * (3 + 2 * sharers),
        out_specs=(VMEM, VMEM),
        scratch_shapes=[pltpu.VMEM((2 * per, 128), F32)],
        name="input_gradient",
        compiler_params=PARAMS,
    )(where, pieces, *own_weights, *near, *there)
    return (saved_key_gradient, saved_value_gradient, cached_input_gradient, grad_span_input)


def solution(mesh):
    split = Mesh(
        mesh.devices.reshape(4, 8, 2, 2, mesh.shape["head"]),
        ("seq_0", "seq_1", "seq_2", "seq_3", "head"),
    )
    in_specs = (
        P(SEQ, "head"),
        P(SEQ, "head"),
        P(SEQ, "head"),
        P(SEQ, "head"),
        P(SEQ),
        P(),
        P(SEQ, "head"),
        P(None, "head"),
        P(None, "head"),
    )
    out_specs = (P(SEQ, "head"), P(SEQ, "head"), P(SEQ, "head"), P("head", SEQ))
    return jax.shard_map(local, mesh=split, in_specs=in_specs, out_specs=out_specs, check_vma=False)
```

```python
import functools

import jax
import jax.numpy as jnp
from jax import lax
from jax.experimental import pallas as pl
from jax.experimental.pallas import tpu as pltpu
from jax.sharding import Mesh
from jax.sharding import PartitionSpec as P

HEAD_WIDTH = 128
SEQ = ("seq_0", "seq_1", "seq_2", "seq_3")
FAR = ("seq_0", "seq_1", "seq_2")
CORE = "seq_3"
LOWEST_SCORE = -1e30
LOWEST_PEAK = -1e29
DEAD = 1e9
SCALE = HEAD_WIDTH ** (-0.5)
F32 = jnp.float32
BF16 = jnp.bfloat16
VMEM = pl.BlockSpec(memory_space=pltpu.VMEM)
PARAMS = pltpu.CompilerParams(vmem_limit_bytes=32 * 1024 * 1024)
SMEM = pl.BlockSpec(memory_space=pltpu.SMEM)


def rows_dot(a, b):
    return lax.dot_general(a, b, (((1,), (1,)), ((), ())), preferred_element_type=F32)


def plain_dot(a, b):
    return lax.dot_general(a, b, (((1,), (0,)), ((), ())), preferred_element_type=F32)


def three_parts(value):
    high = value.astype(BF16).astype(F32)
    rest = value - high
    middle = rest.astype(BF16).astype(F32)
    low = (rest - middle).astype(BF16).astype(F32)
    return high, middle, low


def spread(held):
    axis = held.ndim - 1
    high, middle, low = three_parts(held)
    return high + pltpu.roll(middle, 16, axis) + pltpu.roll(low, 32, axis)


def gathered_parts(block):
    wide = block.astype(F32)
    axis = wide.ndim - 1
    return wide + pltpu.roll(wide, 112, axis) + pltpu.roll(wide, 96, axis)


def pack_kernel(heads, q_ref, g_ref, row_ref):
    lines = []
    for ref in (q_ref, g_ref):
        wide = ref[...].astype(F32)
        lines += [wide[:, h * HEAD_WIDTH : (h + 1) * HEAD_WIDTH] for h in range(heads)]
    lines.append(jnp.zeros((row_ref.shape[1] - 2 * heads, HEAD_WIDTH), F32))
    row = jnp.concatenate(lines, axis=0).astype(BF16)
    for k in range(row_ref.shape[0]):
        row_ref[k] = row


def length_kernel(own_ref, other_ref, row_ref, out_ref, held_ref, sem):
    lane = lax.broadcasted_iota(jnp.int32, (8, 128), 1)
    own, other = own_ref[0], other_ref[0]
    numbers = jnp.where(lane == 0, own // 16, 0) + jnp.where(lane == 1, own % 16, 0)
    numbers += jnp.where(lane == 2, other // 16, 0) + jnp.where(lane == 3, other % 16, 0)
    numbers = numbers.astype(F32).astype(BF16)
    for k in range(held_ref.shape[0]):
        held_ref[k] = numbers
    copy = pltpu.make_async_copy(held_ref, out_ref.at[:, out_ref.shape[1] - 8 :, :], sem)
    copy.start()
    copy.wait()


def first_kernel(heads, group, where_ref, x_ref, k_ref, v_ref, y_ref, place_ref):
    rows = x_ref.shape[0]
    half = k_ref.shape[0] // 2
    far, core, span, row_total = (where_ref[0], where_ref[1], where_ref[2], where_ref[3])
    lens = x_ref[:, 2 * heads :, :].astype(F32)
    lane = lax.broadcasted_iota(jnp.int32, lens.shape, 2)
    row = lax.broadcasted_iota(jnp.int32, lens.shape, 0)
    first_line = lax.broadcasted_iota(jnp.int32, lens.shape, 1) == 0
    lens = lens * jnp.where(first_line & (lane < 4), jnp.where(lane % 2 == 0, 16.0, 1.0), 0.0)
    base = jnp.sum(jnp.where(row < far, lens, 0.0))
    here = jnp.where(row == far, lens, 0.0)
    own = jnp.sum(jnp.where(lane < 2, here, 0.0))
    other = jnp.sum(jnp.where(lane >= 2, here, 0.0))
    is_second = core.astype(F32)
    own_offset = base + is_second * other
    other_offset = base + (1.0 - is_second) * own
    place_ref[0] = own_offset
    place_ref[1] = other_offset
    place_ref[2] = own
    place_ref[3] = other
    within = lax.broadcasted_iota(jnp.int32, (1, half), 1).astype(F32)
    position = jnp.concatenate(
        [
            jnp.where(within < own, own_offset + within, DEAD),
            jnp.where(within < other, other_offset + within, DEAD),
        ],
        axis=1,
    )
    tall = group * heads
    index = lax.broadcasted_iota(jnp.int32, (tall, 1), 0) // heads
    lane = lax.broadcasted_iota(jnp.int32, (tall, 128), 1)
    keys = k_ref[...]
    values = v_ref[...]
    for first in range(0, rows, group):
        part = pl.ds(first, group)
        q = x_ref[part, :heads, :].reshape(tall, HEAD_WIDTH)
        g = x_ref[part, heads : 2 * heads, :].reshape(tall, HEAD_WIDTH)
        asked = (span * row_total + 2 * (first + index) + core).astype(F32)
        scores = jnp.where(position <= asked, rows_dot(q, keys) * SCALE, LOWEST_SCORE)
        peak = jnp.maximum(jnp.max(scores, axis=1, keepdims=True), LOWEST_PEAK)
        raised = jnp.exp(scores - peak)
        grads = rows_dot(g, values)
        total = jnp.sum(raised, axis=1, keepdims=True)
        mean = jnp.sum(raised * grads, axis=1, keepdims=True) / jnp.maximum(total, 0.5)
        moved = (raised * (grads - mean)).astype(BF16)
        both = plain_dot(jnp.concatenate([moved, raised.astype(BF16)], axis=0), keys)
        y_ref[part, :heads, :] = both[:tall].astype(BF16).reshape(group, heads, HEAD_WIDTH)
        y_ref[part, heads : 2 * heads, :] = both[tall:].astype(BF16).reshape(group, heads, HEAD_WIDTH)
        held = jnp.where(lane == 0, peak, jnp.where(lane == 1, total, jnp.where(lane == 2, mean, 0.0)))
        held = spread(held).reshape(group, 2, heads // 2, 128)
        held = held[:, 0] + pltpu.roll(held[:, 1], 64, 2)
        y_ref[part, 2 * heads :, :] = held.astype(BF16)


def merge_kernel(heads, z_ref, u_ref):
    stats = gathered_parts(z_ref[:, 2 * heads :, :])
    total = pltpu.roll(stats, 127, 2)
    mean = pltpu.roll(stats, 126, 2)
    row_peak = jnp.max(stats, axis=0, keepdims=True)
    share = jnp.exp(stats - row_peak)
    part = share * total
    row_total = jnp.sum(part, axis=0, keepdims=True)
    row_mean = jnp.sum(part * mean, axis=0, keepdims=True) / row_total
    moved_factor = share * (SCALE / row_total)
    plain_factor = moved_factor * (mean - row_mean)

    def of_heads(factor):
        return jnp.concatenate([factor[:, :, 0:1], factor[:, :, 64:65]], axis=1)

    term = z_ref[:, :heads, :].astype(F32) * of_heads(moved_factor)
    term += z_ref[:, heads : 2 * heads, :].astype(F32) * of_heads(plain_factor)
    query_grads = jnp.sum(term, axis=0).astype(BF16)
    lane = lax.broadcasted_iota(jnp.int32, (heads // 2, 128), 1) % 64
    found = jnp.where(lane == 0, row_peak[0], 0.0)
    found = jnp.where(lane == 1, pltpu.roll(row_total[0], 1, 1), found)
    found = jnp.where(lane == 2, pltpu.roll(row_mean[0], 2, 1), found)
    found = spread(found).astype(BF16)
    for k in range(u_ref.shape[0]):
        u_ref[k, :heads, :] = query_grads
        u_ref[k, heads:, :] = found


def second_kernel(
    heads, group, where_ref, place_ref, x_ref, u_ref, k_ref, v_ref, w_ref, own_ref, other_ref
):
    rows = x_ref.shape[0]
    slots = k_ref.shape[0]
    half = slots // 2
    core, span, row_total = (where_ref[1], where_ref[2], where_ref[3])
    within = lax.broadcasted_iota(jnp.int32, (half, 1), 0).astype(F32)
    position = jnp.concatenate(
        [
            jnp.where(within < place_ref[2], place_ref[0] + within, DEAD),
            jnp.where(within < place_ref[3], place_ref[1] + within, DEAD),
        ],
        axis=0,
    )
    wide = group * heads
    index = lax.broadcasted_iota(jnp.int32, (1, wide), 1) // heads
    stats = gathered_parts(u_ref[:, heads:, :])
    keys = k_ref[...]
    values = v_ref[...]
    value_grads = jnp.zeros((slots, HEAD_WIDTH), F32)
    key_grads = jnp.zeros((slots, HEAD_WIDTH), F32)
    for first in range(0, rows, group):
        part = pl.ds(first, group)
        q = x_ref[part, :heads, :].reshape(wide, HEAD_WIDTH)
        g = x_ref[part, heads : 2 * heads, :].reshape(wide, HEAD_WIDTH)
        held = stats[first : first + group]
        held = jnp.concatenate([held, pltpu.roll(held, 64, 2)], axis=1).reshape(wide, 128)
        turned = jnp.transpose(held)
        asked = (span * row_total + 2 * (first + index) + core).astype(F32)
        scores = rows_dot(keys, q) * SCALE
        raised = jnp.exp(jnp.where(position <= asked, scores - turned[0:1], LOWEST_SCORE))
        weights = raised * (1.0 / turned[1:2])
        score_grads = weights * (rows_dot(values, g) - turned[2:3])
        value_grads += plain_dot(weights.astype(BF16), g)
        key_grads += plain_dot(score_grads.astype(BF16), q)
    key_grads *= SCALE
    low = jnp.concatenate([u_ref[:, h, :] for h in range(heads)], axis=1)
    features = w_ref.shape[0] // 2
    both = rows_dot(low, w_ref[...])
    for ref, first in ((own_ref, 0), (other_ref, 1)):
        part = slice(first * half, (first + 1) * half)
        ref[:half, :HEAD_WIDTH] = key_grads[part]
        ref[:half, HEAD_WIDTH:] = value_grads[part]
        ref[half:, :] = jnp.zeros((rows, 2 * HEAD_WIDTH), F32)
        ref[half:, :features] = both[:, first * features : (first + 1) * features]


def folded(value):
    high = value.astype(BF16).astype(F32)
    wide = high + pltpu.roll((value - high).astype(BF16).astype(F32), 32, 1)
    count = value.shape[0] // 4
    a, b, c, d = [wide[k * count : (k + 1) * count] for k in range(4)]
    both = [a + pltpu.roll(b, 64, 1), c + pltpu.roll(d, 64, 1)]
    return jnp.concatenate(both, axis=1).astype(BF16)


def unfolded(block):
    wide = block.astype(F32)
    left, right = wide[:, :128], wide[:, 128:]
    rows = [left, pltpu.roll(left, 64, 1), right, pltpu.roll(right, 64, 1)]
    rows = jnp.concatenate(rows, axis=0)
    return rows + pltpu.roll(rows, 96, 1)


def finish_kernel(groups, features, where_ref, own_ref, other_ref, k_ref, v_ref, send_ref):
    half = k_ref.shape[0]
    per = (own_ref.shape[0] - half) // groups
    sums = (own_ref[:half, :] + other_ref[:half, :]).astype(BF16)
    k_ref[...] = sums[:, :HEAD_WIDTH]
    v_ref[...] = sums[:, HEAD_WIDTH:]
    is_first = where_ref[1] == 0
    lane = lax.broadcasted_iota(jnp.int32, (2 * per, 128), 1)
    for target in range(groups):
        part = slice(half + per * target, half + per * (target + 1))
        mine, theirs = own_ref[part, :128], other_ref[part, :128]
        even = jnp.where(is_first, mine, theirs)
        odd = jnp.where(is_first, theirs, mine)
        lines = jnp.where(lane < features, jnp.concatenate([even, odd], axis=0), 0.0)
        send_ref[target, :half, :] = sums
        send_ref[target, half:, :] = folded(lines)


def input_kernel(groups, sharers, where_ref, arrived_ref, own_k_ref, own_v_ref, *refs):
    here, there, refs = refs[:sharers], refs[sharers : 2 * sharers], refs[2 * sharers :]
    out_ref, block_ref, turn_ref = refs
    half = out_ref.shape[0]
    is_first = where_ref[1] == 0
    mine = where_ref[4]
    left = [arrived_ref[mine, :half, :]]
    span = unfolded(arrived_ref[0, half:, :])
    for k in range(1, groups):
        both = arrived_ref[lax.rem(mine - k + groups, groups), :half, :]
        keys, values = both[:, :HEAD_WIDTH], both[:, HEAD_WIDTH:]
        left += [jnp.where(is_first, keys, values), jnp.where(is_first, values, keys)]
        span += unfolded(arrived_ref[k, half:, :])
    left = jnp.concatenate(left, axis=1)
    share = out_ref.shape[1] // sharers
    for k, (near_ref, far_ref) in enumerate(zip(here, there)):
        start = lax.rem(where_ref[5] - k + sharers, sharers) * share
        part = pl.ds(pl.multiple_of(start, share), share)
        right = [own_k_ref[part, :], own_v_ref[part, :]]
        for other in range(groups - 1):
            lines = slice(other * share, (other + 1) * share)
            right += [near_ref[lines, :], far_ref[lines, :]]
        out_ref[:, part] = rows_dot(left, jnp.concatenate(right, axis=1)).astype(BF16)
    rows, features = block_ref.shape
    turn_ref[pl.ds(0, rows // 2, stride=2), :] = span[: rows // 2]
    turn_ref[pl.ds(1, rows // 2, stride=2), :] = span[rows // 2 :]
    block_ref[...] = turn_ref[:, :features].astype(BF16)


def exchanged(value, axes):
    return lax.all_to_all(value, axes, split_axis=0, concat_axis=0, tiled=True)


def shifted(value, axis, by):
    count = lax.axis_size(axis)
    return lax.ppermute(value, axis, [(k, (k + by) % count) for k in range(count)])


def local(
    queries,
    grad_output,
    key_cache,
    saved_value_rows,
    lengths,
    span_index,
    w_query,
    key_projection_weight,
    value_projection_weight,
):
    heads = queries.shape[1] // HEAD_WIDTH
    rows = lax.axis_size(FAR)
    block = key_cache.shape[0]
    groups = lax.axis_size("head")
    core = lax.axis_index(CORE)
    far = lax.axis_index(FAR)
    mine = lax.axis_index("head")
    lines = 2 * heads + 8
    group = min(16, rows)

    other_length = shifted(lengths, CORE, 1)
    pack_call = pl.pallas_call(
        functools.partial(pack_kernel, heads),
        out_shape=jax.ShapeDtypeStruct((rows, lines, HEAD_WIDTH), BF16),
        in_specs=[VMEM, VMEM],
        out_specs=VMEM,
        name="row_pack",
    )
    row = pack_call(queries, grad_output)
    row = pl.pallas_call(
        length_kernel,
        out_shape=jax.ShapeDtypeStruct(row.shape, BF16),
        in_specs=[SMEM, SMEM, pl.BlockSpec(memory_space=pl.ANY)],
        out_specs=pl.BlockSpec(memory_space=pl.ANY),
        scratch_shapes=[pltpu.VMEM((rows, 8, HEAD_WIDTH), BF16), pltpu.SemaphoreType.DMA],
        input_output_aliases={2: 0},
        name="row_lengths",
    )(lengths, other_length, row)
    x = exchanged(row, FAR)

    cache = jnp.concatenate([key_cache, saved_value_rows], axis=1)
    other_cache = shifted(cache, CORE, 1)
    keys = jnp.concatenate([key_cache, other_cache[:, :HEAD_WIDTH]], axis=0)
    values = jnp.concatenate([saved_value_rows, other_cache[:, HEAD_WIDTH:]], axis=0)

    features = key_projection_weight.shape[0] // groups
    sharers = lax.axis_size("seq_0")
    share = features // sharers
    first_is_key = core == 0
    half_weights = jnp.where(first_is_key, key_projection_weight, value_projection_weight)
    arriving = []
    for k in range(1, groups):
        start = lax.rem(mine + k, groups) * features + lax.axis_index("seq_0") * share
        piece = lax.dynamic_slice_in_dim(half_weights, start, share, 0)
        arriving.append(shifted(piece, "head", k))
    near = [jnp.concatenate(arriving, axis=0)]
    for k in range(1, sharers):
        near.append(shifted(near[0], "seq_0", k))
    there = []
    for piece in near:
        there.append(shifted(piece, CORE, 1))
    own_weights = [
        lax.dynamic_slice_in_dim(w, mine * features, features, 0)
        for w in (key_projection_weight, value_projection_weight)
    ]
    other_query = shifted(w_query, CORE, 1)
    both_query = jnp.concatenate([w_query, other_query], axis=0)

    where = jnp.full((8,), 2 * rows, jnp.int32)
    for k, number in ((0, far), (1, core), (2, span_index[0]), (4, mine), (5, lax.axis_index("seq_0"))):
        where = jnp.where(jnp.arange(8) == k, number, where)
    y, place = pl.pallas_call(
        functools.partial(first_kernel, heads, group),
        out_shape=(
            jax.ShapeDtypeStruct((rows, lines, HEAD_WIDTH), BF16),
            jax.ShapeDtypeStruct((4,), F32),
        ),
        in_specs=[SMEM, VMEM, VMEM, VMEM],
        out_specs=(VMEM, SMEM),
        name="row_partials",
        compiler_params=PARAMS,
    )(where, x, keys, values)
    arrived = exchanged(y, FAR)
    merged = pl.pallas_call(
        functools.partial(merge_kernel, heads),
        out_shape=jax.ShapeDtypeStruct((rows, heads + 8, HEAD_WIDTH), BF16),
        in_specs=[VMEM],
        out_specs=VMEM,
        name="row_merge",
        compiler_params=PARAMS,
    )(arrived)
    u = exchanged(merged, FAR)
    width = w_query.shape[0]
    own_part, other_part = pl.pallas_call(
        functools.partial(second_kernel, heads, group),
        out_shape=(jax.ShapeDtypeStruct((block + rows, 2 * HEAD_WIDTH), F32),) * 2,
        in_specs=[SMEM, SMEM, VMEM, VMEM, VMEM, VMEM, VMEM],
        out_specs=(VMEM, VMEM),
        name="slot_gradients",
        compiler_params=PARAMS,
    )(where, place, x, u, keys, values, both_query)
    other_sums = shifted(other_part, CORE, 1)
    per = rows // groups
    saved_key_gradient, saved_value_gradient, leaving = pl.pallas_call(
        functools.partial(finish_kernel, groups, width),
        out_shape=(
            jax.ShapeDtypeStruct((block, HEAD_WIDTH), BF16),
            jax.ShapeDtypeStruct((block, HEAD_WIDTH), BF16),
            jax.ShapeDtypeStruct((groups, block + per // 2, 2 * HEAD_WIDTH), BF16),
        ),
        in_specs=[SMEM, VMEM, VMEM],
        out_specs=(VMEM, VMEM, VMEM),
        name="slot_sums",
        compiler_params=PARAMS,
    )(where, own_part, other_sums)

    pieces = exchanged(leaving, "head")
    cached_input_gradient, grad_span_input = pl.pallas_call(
        functools.partial(input_kernel, groups, sharers),
        out_shape=(
            jax.ShapeDtypeStruct((block, features), BF16),
            jax.ShapeDtypeStruct((2 * per, width), BF16),
        ),
        in_specs=[SMEM] + [VMEM] * (3 + 2 * sharers),
        out_specs=(VMEM, VMEM),
        scratch_shapes=[pltpu.VMEM((2 * per, 128), F32)],
        name="input_gradient",
        compiler_params=PARAMS,
    )(where, pieces, *own_weights, *near, *there)
    return (saved_key_gradient, saved_value_gradient, cached_input_gradient, grad_span_input)


def solution(mesh):
    split = Mesh(
        mesh.devices.reshape(4, 8, 2, 2, mesh.shape["head"]),
        ("seq_0", "seq_1", "seq_2", "seq_3", "head"),
    )
    in_specs = (
        P(SEQ, "head"),
        P(SEQ, "head"),
        P(SEQ, "head"),
        P(SEQ, "head"),
        P(SEQ),
        P(),
        P(SEQ, "head"),
        P(None, "head"),
        P(None, "head"),
    )
    out_specs = (P(SEQ, "head"), P(SEQ, "head"), P(SEQ, "head"), P("head", SEQ))
    return jax.shard_map(local, mesh=split, in_specs=in_specs, out_specs=out_specs, check_vma=False)
```
